128 devices in a mesh: leaf: 128 (over x, y, z, core).
Axes of the slice: x: 4, y: 4, z: 4, core: 2. Of those that a mesh axis runs over, the one named last changes fastest.
Arguments:
- x_vecs: bfloat16 [16, 1048576], P(None, 'leaf'), may hold values from -6 to 6
- leaf_basis: bfloat16 [16384, 4096], P('leaf'), may hold values from -0.75 to 0.75
- near_blocks: bfloat16 [16384, 12288], P('leaf'), may hold values from -0.4375 to 0.4375
- local_edges: float32 [32512, 4096], P('leaf'), may hold values from -0.5 to 0.5
- top_edges: float32 [128, 6, 4096], P('leaf'), may hold values from -1 to 1, as said below
- top_couple: float32 [128, 7, 4096], P('leaf'), may hold values from -3 to 3, as said below
- couple_blocks: bfloat16 [65536, 4096], P('leaf'), may hold values from -0.75 to 0.75
- couple_src: int32 [65536], P('leaf'), may hold values from 0 to 127
- couple_owner: int32 [65536, 1], P('leaf'), may hold values from 0 to 127; in each aligned block of 512 rows (0 to 511, 512 to 1023, ...) at most 8 rows name the same one
- couple_dst: int32 [65536], P('leaf'), may hold values from 0 to 127
Outputs:
- y_vecs: float32 [16, 1048576], P(None, 'leaf')
The draws below stay inside these ranges and needn't reach their ends.
Inputs may be any that keep to these rules, and one draw needn't show every extreme that they name: `couple_owner`: the rows of one device name each owner at most 8 times, a bound that some block reaches. top_edges[o, b] belongs to the level-b cluster that holds device o and is the same for all devices of that cluster. top_couple[o, b] belongs to the level-b cluster that holds device o and is the same for all devices of that cluster.
All inputs are finite; a program needn't handle non-finite values.
Results may differ from the reference program's by a relative error of at most 0.0044.
Values may be sent and summed in bfloat16 or wider, within the bound.
No kernel may reach another device: no remote copies, remote signals or barrier semaphores. Data moves between devices by JAX's collectives and lax.ppermute only.
A program may use at most 128 MiB of HBM per device.

```python
import math
import jax
import jax.numpy as jnp
import numpy as np
from jax import lax

LEAF = 64
RANK = 64
NV = 16
LEAF_DEV = 128
OWNERS = 128
TOPLV = 7
TOPE = 6
LEAVES = 16384
POINTS = 1048576
EDGES = 32512
PAIRS_DEV = 512
PAIRS = 65536
CAP = 8


def spread_levels(key, depth_count, spread):
    raw_values = jnp.clip(jax.random.normal(key, (OWNERS, depth_count, RANK * RANK), jnp.float32), -3.0, 3.0) * spread
    owner_ids = jnp.arange(OWNERS, dtype=jnp.int32)
    columns = []
    for depth in range(depth_count):
        leading = owner_ids // 2 ** depth * 2 ** depth
        columns.append(raw_values[leading, depth])
    return jnp.stack(columns, axis=1)


def draw_top_edges(key, part):
    return spread_levels(jax.random.fold_in(key, 11), TOPE, (2.0 * RANK) ** (-0.5))


def draw_top_couple(key, part):
    return spread_levels(jax.random.fold_in(key, 23), TOPLV, 3.0 * RANK ** (-0.5))


def with_ends(array, key, smallest, largest):
    place = [jax.random.randint(jax.random.fold_in(key, axis), (), 0, length) for axis, length in enumerate(array.shape)]
    main_axis = array.shape.index(max(array.shape))
    beside = place[:main_axis] + [(place[main_axis] + 1) % array.shape[main_axis]] + place[main_axis + 1:]
    return array.at[tuple(place)].set(smallest).at[tuple(beside)].set(largest)


def shard_levels(stream_key, shape, shards, least, largest):
    gain, own = 1.0, jax.random.fold_in(stream_key, 6)
    for dim, parts in shards:
        heights = jnp.exp(jax.random.uniform(jax.random.fold_in(own, dim), (parts,), jnp.float32, least / len(shards), largest / len(shards)))
        gain = gain * jnp.repeat(heights, shape[dim] // parts).reshape([-1 if axis == dim else 1 for axis in range(len(shape))])
    return gain


def assign_block(key, own, number, rows, amount, top, limit, skew):
    sequence = jax.random.permutation(key, amount)
    packed, ordinary = portions_of(amount, rows * top, limit, skew, True), portions_of(amount, rows * top, limit, skew, False)
    places = jnp.arange(amount)

    def named(lengths, turn):
        used = int((lengths > 0).sum())
        fixed = max(1, used // 4)
        passed = fixed + (places - fixed + turn * (used - fixed)) % max(1, amount - fixed)
        return jnp.zeros((amount,), jnp.int32).at[sequence[jnp.where(places < fixed, places, passed)]].set(jnp.asarray(lengths, jnp.int32))

    lengths = jnp.where(number % 4 == 0, named(packed, number // 4), named(ordinary, number - number // 4 - 1))
    mixed = jax.random.permutation(jax.random.fold_in(own, 3), amount)
    donor, taker = mixed[0:amount // 2 * 2:2], mixed[1:amount // 2 * 2:2]
    margin = jnp.minimum(lengths[donor] - 1, limit - lengths[taker]) // 2
    margin = jnp.where((donor == sequence[0]) | (taker == sequence[0]) | (lengths[taker] == 0), 0, jnp.maximum(margin, 0))
    passed = jax.random.randint(jax.random.fold_in(own, 4), (amount // 2,), 0, 1 << 20) % (margin + 1)
    lengths = lengths.at[donor].add(-passed).at[taker].add(passed)
    labels = jnp.searchsorted(jnp.cumsum(lengths), jnp.arange(rows * top), side="right").astype(jnp.int32)
    table = labels.reshape(top, rows).T
    table = table[jax.random.permutation(jax.random.fold_in(own, 1), rows)]
    turn = jax.random.randint(jax.random.fold_in(own, 2), (rows, 1), 0, top)
    return jnp.take_along_axis(table, (jnp.arange(top)[None, :] + turn) % top, axis=1)


def portions_of(amount, total, limit, slope, full):
    weights = [(1 << 20) // math.isqrt(rank ** slope) + 1 for rank in range(1, amount + 1)]
    largest = limit if full else min(limit, max(-(-total // amount), total * weights[0] // sum(weights)))
    least = 1 if total - largest >= amount - 1 else 0
    holding, surplus = [largest] + [least] * (amount - 1), total - largest - least * (amount - 1)
    while surplus > 0:
        movable = [i for i in range(1, amount) if holding[i] < largest] or [i for i in range(1, amount) if holding[i] < limit]
        whole, left = sum([weights[i] for i in movable]), surplus
        for i in movable:
            addition = min(limit - holding[i], max(1, left * weights[i] // whole), surplus)
            holding[i] = holding[i] + addition
            surplus = surplus - addition
    return np.array(holding)


def bell_draw(rng, shape, deviation, most, pieces=(), kind=jnp.bfloat16):
    loudness = shard_levels(rng, shape, pieces, -0.22, 0.18) if pieces else 1.0
    drawn = jax.random.normal(rng, shape, jnp.float32) * deviation * loudness
    return jnp.minimum(jnp.maximum(drawn, -most), most).astype(kind)


def setup_inputs(seed: int = 0) -> dict:
    streams_of = jax.random.split(jax.random.key(seed), 11)
    x_vecs = bell_draw(streams_of[0], (NV, POINTS), 1.0, 6.0, ((1, 128),))
    leaf_basis = bell_draw(streams_of[1], (LEAVES, LEAF * RANK), LEAF ** -0.5, 0.75, ((0, 128),))
    near_blocks = bell_draw(streams_of[2], (LEAVES, 3 * LEAF * LEAF), (3 * LEAF) ** -0.5, 0.4375, ((0, 128),))
    local_edges = bell_draw(streams_of[3], (EDGES, RANK * RANK), (2 * RANK) ** -0.5, 0.5, ((0, 128),), jnp.float32)
    top_edges = draw_top_edges(jax.random.fold_in(streams_of[10], 71), 0)
    top_couple = draw_top_couple(jax.random.fold_in(streams_of[10], 71), 0)
    couple_blocks = bell_draw(streams_of[6], (PAIRS, RANK * RANK), RANK ** -0.5, 0.75, ((0, 128),))
    couple_src = with_ends(jax.random.randint(streams_of[7], (PAIRS,), 0, LEAF_DEV), jax.random.fold_in(streams_of[7], 1), 0, LEAF_DEV - 1).astype(jnp.int32)
    couple_owner_keys = jax.random.split(jax.random.fold_in(streams_of[8], 1), PAIRS // PAIRS_DEV)
    couple_owner_turns = jax.random.permutation(jax.random.fold_in(streams_of[8], 3), PAIRS // PAIRS_DEV)
    couple_owner = jax.vmap(lambda own, number: assign_block(jax.random.fold_in(streams_of[8], 2), own, number, PAIRS_DEV, OWNERS, 1, CAP, 2))(couple_owner_keys, couple_owner_turns).reshape((PAIRS, 1))
    couple_dst = with_ends(jax.random.randint(streams_of[9], (PAIRS,), 0, LEAF_DEV), jax.random.fold_in(streams_of[9], 1), 0, LEAF_DEV - 1).astype(jnp.int32)
    return {"x_vecs": x_vecs, "leaf_basis": leaf_basis, "near_blocks": near_blocks, "local_edges": local_edges, "top_edges": top_edges, "top_couple": top_couple, "couple_blocks": couple_blocks, "couple_src": couple_src, "couple_owner": couple_owner, "couple_dst": couple_dst}


exact_prec = lax.Precision.HIGHEST


def reference(x_vecs, leaf_basis, near_blocks, local_edges, top_edges, top_couple, couple_blocks, couple_src, couple_owner, couple_dst):
    vec_leaves = x_vecs.reshape(NV, LEAVES, LEAF).astype(jnp.float32)
    bases_all = leaf_basis.reshape(LEAVES, LEAF, RANK).astype(jnp.float32)
    coeffs = jnp.einsum('vtp,tpk->tvk', vec_leaves, bases_all)
    coeff_round = coeffs.astype(jnp.bfloat16)
    edge_mats = local_edges.reshape(OWNERS, 2 * LEAF_DEV - 2, RANK, RANK)
    states = coeffs.reshape(OWNERS, LEAF_DEV, NV, RANK)
    offset = 0
    nodes_now = LEAF_DEV
    while nodes_now > 1:
        chosen = edge_mats[:, offset:offset + nodes_now]
        carried = jnp.einsum('onvk,onkl->onvl', states, chosen, precision=exact_prec)
        carried = carried.reshape(OWNERS, nodes_now // 2, 2, NV, RANK)
        states = carried[:, :, 0] + carried[:, :, 1]
        offset = offset + nodes_now
        nodes_now = nodes_now // 2
    root_coeff = states[:, 0]
    top_coeff = [root_coeff]
    for section_no in range(TOPLV - 1):
        stride = 2 ** section_no
        chosen = top_edges[::stride, section_no].reshape(-1, RANK, RANK)
        carried = jnp.einsum('mvk,mkl->mvl', top_coeff[-1], chosen, precision=exact_prec)
        carried = carried.reshape(-1, 2, NV, RANK)
        top_coeff.append(carried[:, 0] + carried[:, 1])
    top_down = jnp.zeros((1, NV, RANK), jnp.float32)
    for section_no in reversed(range(TOPLV)):
        stride = 2 ** section_no
        current = top_coeff[section_no]
        nodes_here = current.shape[0]
        sibling = current.reshape(nodes_here // 2, 2, NV, RANK)[:, ::-1].reshape(nodes_here, NV, RANK)
        coupling = top_couple[::stride, section_no].reshape(nodes_here, RANK, RANK)
        result = jnp.einsum('mvl,mkl->mvk', sibling, coupling, precision=exact_prec)
        if section_no < TOPLV - 1:
            parent = jnp.repeat(top_down, 2, axis=0)
            chosen = top_edges[::stride, section_no].reshape(nodes_here, RANK, RANK)
            result = result + jnp.einsum('mvl,mkl->mvk', parent, chosen, precision=exact_prec)
        top_down = result
    states = top_down[:, None]
    nodes_now = 1
    while nodes_now < LEAF_DEV:
        nodes_now = nodes_now * 2
        offset = 2 * LEAF_DEV - 2 * nodes_now
        chosen = edge_mats[:, offset:offset + nodes_now]
        parent = jnp.repeat(states, 2, axis=1)
        states = jnp.einsum('onvl,onkl->onvk', parent, chosen, precision=exact_prec)
    leaf_down = states.reshape(LEAVES, NV, RANK)
    pair_ids = jnp.arange(PAIRS, dtype=jnp.int32)
    src_global = (pair_ids // PAIRS_DEV) * LEAF_DEV + couple_src
    dst_global = couple_owner[:, 0] * LEAF_DEV + couple_dst
    picked = coeff_round[src_global].astype(jnp.float32)
    pair_mats = couple_blocks.reshape(PAIRS, RANK, RANK).astype(jnp.float32)
    pair_round = jnp.einsum('pvl,pkl->pvk', picked, pair_mats).astype(jnp.bfloat16)
    pair_round = lax.optimization_barrier(pair_round)
    far_sum = jax.ops.segment_sum(pair_round.astype(jnp.float32), dst_global, num_segments=LEAVES)
    leaf_hat = (leaf_down + far_sum).astype(jnp.bfloat16)
    blocks = near_blocks.reshape(LEAVES, 3, LEAF, LEAF).astype(jnp.float32)
    before = jnp.roll(vec_leaves, 1, axis=1)
    following = jnp.roll(vec_leaves, -1, axis=1)
    near_part = jnp.einsum('vtq,tpq->vtp', before, blocks[:, 0])
    near_part = near_part + jnp.einsum('vtq,tpq->vtp', vec_leaves, blocks[:, 1])
    near_part = near_part + jnp.einsum('vtq,tpq->vtp', following, blocks[:, 2])
    far_part = jnp.einsum('tvk,tpk->vtp', leaf_hat.astype(jnp.float32), bases_all)
    return (far_part + near_part).reshape(NV, POINTS)
```

```python
import jax
import jax.numpy as jnp
from jax import lax
from jax.experimental import pallas as pl
from jax.experimental.pallas import tpu as pltpu
from jax.sharding import PartitionSpec as P

LEAF = 64
RANK = 64
NV = 16
LEAF_DEV = 128
PEERS = 128
LEVELS = 7
SLOTS = 8
TILES = SLOTS + 2
PAIR_ROWS = 512
EDGE_ROWS = 254
FLAT = 4096
HALF = 64
VMEM_LIMIT = 60 * 1024 * 1024

LEVEL_BASE = {128: 0, 64: 64, 32: 96, 16: 112, 8: 120, 4: 124, 2: 126}

f32 = jnp.float32
bf16 = jnp.bfloat16


def low_lanes(rows):
    return lax.broadcasted_iota(jnp.int32, (rows, 128), 1) < HALF


def half_masks(rows):
    low = low_lanes(rows).astype(f32)
    return low.astype(bf16), (1.0 - low).astype(bf16)


def swap(value):
    return pltpu.roll(value, HALF, 1)


def join(first, second):
    return jnp.where(low_lanes(first.shape[0]), first, swap(second))


def split(value):
    high = value.astype(bf16)
    return high, (value - high.astype(f32)).astype(bf16)


def mm(left, right):
    return jnp.dot(left, right, preferred_element_type=f32)


def mmt(left, right):
    return lax.dot_general(left, right, (((1,), (1,)), ((), ())), preferred_element_type=f32)


def paired(stage, group, load_first, load_second):
    low = low_lanes(group)
    for j in range(32):
        first = load_first(j)
        second = load_second(j)
        stage[pl.ds(2 * j * group, group), :] = jnp.where(low, first, swap(second))
        stage[pl.ds((2 * j + 1) * group, group), :] = jnp.where(low, swap(first), second)


def matrix(stage, group, index):
    return stage[pl.ds(index, 64, stride=group), :]


def lanes(j, start=0):
    return pl.ds(start + j * 128, 128)


def relayout_edges(edges, stage, highs, lows):
    def keep(index, place):
        high, low = split(matrix(stage, 8, index))
        highs[place] = high
        lows[place] = low

    def group(g, _):
        first = jnp.where(
            g < 8, 8 * g, jnp.where(g < 12, 64 + 8 * g, jnp.where(g < 14, 96 + 8 * g, 224))
        )
        gap = jnp.where(g < 8, 64, jnp.where(g < 12, 32, jnp.where(g < 14, 16, 8)))
        first = pl.multiple_of(first, 8)
        second = pl.multiple_of(first + gap, 8)
        paired(
            stage,
            8,
            lambda j: edges[pl.ds(first, 8), lanes(j)],
            lambda j: edges[pl.ds(second, 8), lanes(j)],
        )
        for i in range(8):
            keep(i, 8 * g + i)
        return 0

    lax.fori_loop(0, 15, group, 0)
    paired(
        stage,
        8,
        lambda j: edges[240:248, lanes(j)],
        lambda j: pltpu.roll(edges[240:248, lanes(j)], 4, 0),
    )
    for i in range(4):
        keep(i, 120 + i)
    rows = lax.broadcasted_iota(jnp.int32, (8, 128), 0)

    def last_second(j):
        tile = edges[246:254, lanes(j)]
        return jnp.where(rows < 6, pltpu.roll(tile, 6, 0), pltpu.roll(tile, 7, 0))

    paired(stage, 8, lambda j: edges[246:254, lanes(j)], last_second)
    keep(2, 124)
    keep(3, 125)
    keep(6, 126)


def up_kernel(
    me_ref, src_ref, own_ref, dst_ref, x_ref, basis_hbm, edges_hbm, top_ref, pairs_hbm,
    out_ref, done_ref,
    basis, edges, pairs, stage, vec_a, vec_b, highs, lows, table, rows_at, count, sems,
):
    copies = [
        pltpu.make_async_copy(basis_hbm, basis, sems.at[0]),
        pltpu.make_async_copy(edges_hbm, edges, sems.at[1]),
        pltpu.make_async_copy(pairs_hbm, pairs, sems.at[2]),
    ]
    for copy in copies:
        copy.start()
    low16, high16 = half_masks(16)
    low = low_lanes(16)

    def clear(i, _):
        out_ref[pl.ds(i * 16, 16)] = jnp.zeros((16, 8, 128), bf16)
        return 0

    lax.fori_loop(0, PEERS * TILES // 16, clear, 0)
    rows_at[...] = jnp.zeros_like(rows_at)

    def clear_count(i, _):
        count[i] = 0
        return 0

    lax.fori_loop(0, PEERS, clear_count, 0)

    copies[0].wait()

    def leaf_group(g, _):
        first = pl.multiple_of(16 * g, 16)
        second = pl.multiple_of(64 + 16 * g, 16)
        paired(
            stage,
            16,
            lambda j: basis[pl.ds(first, 16), lanes(j)].astype(f32),
            lambda j: basis[pl.ds(second, 16), lanes(j)].astype(f32),
        )
        for i in range(0, 16, 2):
            weight = jnp.concatenate([matrix(stage, 16, i), matrix(stage, 16, i + 1)], axis=0)
            at = pl.multiple_of(g * 1024 + i * 64, 128)
            left = x_ref[:, pl.ds(at, 128)]
            right = x_ref[:, pl.ds(pl.multiple_of(at + FLAT, 128), 128)]
            stacked = jnp.concatenate(
                [left * low16, right * low16, left * high16, right * high16], axis=0
            )
            found = mm(stacked, weight.astype(bf16))
            for k in range(2):
                pair = jnp.where(low, found[32 * k : 32 * k + 16], found[32 * k + 16 : 32 * k + 32])
                turned = swap(pair)
                t = 16 * g + i + k
                vec_a[t] = pair
                table[t] = jnp.where(low, pair, turned).astype(bf16)
                table[t + 64] = jnp.where(low, turned, pair).astype(bf16)
        return 0

    lax.fori_loop(0, 4, leaf_group, 0)

    copies[1].wait()
    relayout_edges(edges, stage, highs, lows)

    here, there = vec_a, vec_b
    nodes = LEAF_DEV
    while nodes > 2:
        base = LEVEL_BASE[nodes]

        def parent(q, here=here, there=there, base=base):
            p0 = here[2 * q]
            p1 = here[2 * q + 1]
            both = jnp.concatenate(
                [jnp.where(low, p0, swap(p1)), jnp.where(low, swap(p0), p1)], axis=0
            )
            vh, vl = split(both)
            wh = highs[pl.ds(base + 2 * q, 2)].reshape(128, 128)
            wl = lows[pl.ds(base + 2 * q, 2)].reshape(128, 128)
            two = mm(jnp.concatenate([vh, vl], axis=0), wh)
            found = two[:32] + two[32:] + mm(vh, wl)
            there[q] = jnp.where(low, found[:16], found[16:])

        quarter = nodes // 4
        if quarter > 8:

            def block(i, _, parent=parent):
                for k in range(8):
                    parent(8 * i + k)
                return 0

            lax.fori_loop(0, quarter // 8, block, 0)
        else:
            for q in range(quarter):
                parent(q)
        here, there = there, here
        nodes //= 2
    last = here[0]
    both = jnp.concatenate([last, swap(last)], axis=0)[:, :HALF]
    vh, vl = split(both)
    wh = highs[126]
    two = mm(jnp.concatenate([vh, vl], axis=0), wh)
    found = two[:32] + two[32:] + mm(vh, lows[126])
    current = found[:16] + swap(found[16:])

    for j in range(32):
        tile = top_ref[:, lanes(j)]
        stage[pl.ds(16 * j, LEVELS - 1), :] = tile
        stage[pl.ds(16 * j + 8, LEVELS - 1), :] = swap(tile)
    me = me_ref[0]
    for level in range(LEVELS):
        tile = join(current[0:8], current[8:16]).astype(bf16)
        for x in range(2**level, 2 ** (level + 1)):
            out_ref[lax.bitwise_xor(me, x) * TILES + SLOTS] = tile
        if level < LEVELS - 1:
            wh, wl = split(matrix(stage, 8, level))
            vh, vl = split(current[:, :HALF])
            two = mm(jnp.concatenate([vh, vl], axis=0), wh)
            current = two[:16] + two[16:] + mm(vh, wl)

    copies[2].wait()
    lane_ids = lax.broadcasted_iota(jnp.int32, (1, 128), 1)

    def pair_group(g, _):
        first = pl.multiple_of(32 * g, 16)
        second = pl.multiple_of(32 * g + 16, 16)
        paired(
            stage,
            16,
            lambda j: pairs[pl.ds(first, 16), lanes(j)].astype(f32),
            lambda j: pairs[pl.ds(second, 16), lanes(j)].astype(f32),
        )
        for i in range(16):
            weight = matrix(stage, 16, i).astype(bf16)
            listed = [32 * g + i, 32 * g + 16 + i]
            stacked = jnp.concatenate(
                [table[src_ref[listed[0]]] * low16, table[src_ref[listed[1]]] * high16], axis=0
            )
            found = mmt(stacked, weight)
            for k in range(2):
                owner = own_ref[listed[k]]
                rank = count[owner]
                count[owner] = rank + 1
                tile = jnp.concatenate(
                    [found[16 * k : 16 * k + 8], found[16 * k + 8 : 16 * k + 16]], axis=1
                )
                out_ref[owner * TILES + rank] = tile.astype(bf16)
                rows_at[pl.ds(owner * SLOTS + rank, 1), :] = jnp.where(
                    lane_ids == dst_ref[listed[k]], 1.0, 0.0
                )
        return 0

    lax.fori_loop(0, PAIR_ROWS // 32, pair_group, 0)

    def place_rows(o, _):
        out_ref[o * TILES + SLOTS + 1] = rows_at[
            pl.ds(pl.multiple_of(o * SLOTS, 8), 8), :
        ].astype(bf16)
        return 0

    lax.fori_loop(0, PEERS, place_rows, 0, unroll=8)
    done_ref[...] = current[0:8]


def mid_kernel(
    after_ref, xs_ref, xe_ref, near_hbm, basis_hbm, edges_hbm, top_ref,
    near_ref, down_ref, basis_ref, top_out_ref,
    near, basis, edges, stage, stage_two, vec_a, vec_b, highs, lows, sems,
):
    copies = [
        pltpu.make_async_copy(near_hbm, near, sems.at[0]),
        pltpu.make_async_copy(basis_hbm, basis, sems.at[1]),
        pltpu.make_async_copy(edges_hbm, edges, sems.at[2]),
    ]
    for copy in copies:
        copy.start()
    low16, _ = half_masks(16)
    low64, high64 = half_masks(64)
    flow = low_lanes(128)

    copies[0].wait()

    def near_group(g, _):
        first = pl.multiple_of(16 * g, 16)
        rows = pl.ds(first, 16)
        paired(
            stage,
            16,
            lambda j: near[rows, lanes(j)].astype(f32),
            lambda j: near[rows, lanes(j, FLAT)].astype(f32),
        )
        for j in range(32):
            tile = near[rows, lanes(j, 2 * FLAT)].astype(f32)
            stage_two[pl.ds(32 * j, 16), :] = tile
            stage_two[pl.ds(32 * j + 16, 16), :] = swap(tile)
        for i in range(0, 16, 2):
            at = pl.multiple_of(g * 1024 + i * 64, 128)
            after = pl.multiple_of(at + 128, 128)
            found = []
            for k, ref in enumerate((xs_ref, xe_ref)):
                weight = jnp.concatenate(
                    [matrix(stage, 16, i + k), matrix(stage_two, 16, i + k)], axis=1
                ).astype(bf16)
                vec = jnp.concatenate(
                    [ref[:, pl.ds(at, 128)], ref[:, pl.ds(after, 128)] * low16], axis=1
                )
                found.append(mmt(vec, weight))
            near_ref[:, pl.ds(at, 128)] = jnp.concatenate(found, axis=1)
        return 0

    lax.fori_loop(0, 8, near_group, 0)

    copies[1].wait()
    even = (lax.broadcasted_iota(jnp.int32, (16, 128), 0) % 2) == 0

    def basis_group(g, _):
        rows = pl.ds(pl.multiple_of(16 * g, 16), 16)
        for j in range(32):
            tile = basis[rows, lanes(j)].astype(f32)
            turned = swap(tile)
            stage[pl.ds(32 * j, 16), :] = jnp.where(even, tile, turned)
            stage[pl.ds(32 * j + 16, 16), :] = jnp.where(even, turned, tile)
        for i in range(16):
            at = pl.multiple_of(g * 1024 + i * 64, 64)
            value = matrix(stage, 16, i).astype(bf16)
            basis_ref[pl.ds(at, 64), :] = value * (high64 if i % 2 else low64)
        return 0

    lax.fori_loop(0, 8, basis_group, 0)

    copies[2].wait()
    relayout_edges(edges, stage, highs, lows)
    vec_a[0] = highs[126].astype(f32) + lows[126].astype(f32)
    here, there = vec_a, vec_b
    nodes = 4
    while nodes <= LEAF_DEV:
        base = LEVEL_BASE[nodes]

        def children(q, here=here, there=there, base=base, final=nodes == LEAF_DEV):
            ph, plow = split(here[q])
            rh = jnp.concatenate([ph * low64, ph * high64], axis=0)
            rl = jnp.concatenate([plow * low64, plow * high64], axis=0)
            wh = highs[pl.ds(base + 2 * q, 2)].reshape(128, 128)
            wl = lows[pl.ds(base + 2 * q, 2)].reshape(128, 128)
            found = mm(wh, rh) + mm(wl, rh) + mm(wh, rl)
            if not final:
                there[2 * q] = found[:64]
                there[2 * q + 1] = found[64:]
            else:
                high = found.astype(bf16).astype(f32)
                rest = found - high
                at = pl.multiple_of(q * 128, 128)
                down_ref[pl.ds(at, 128), :] = jnp.where(flow, high, swap(rest)).astype(bf16)
                at = pl.multiple_of(q * 128 + FLAT, 128)
                down_ref[pl.ds(at, 128), :] = jnp.where(flow, swap(high), rest).astype(bf16)

        quarter = nodes // 4
        if quarter > 4:

            def block(i, _, children=children):
                for k in range(4):
                    children(4 * i + k)
                return 0

            lax.fori_loop(0, quarter // 4, block, 0)
        else:
            for q in range(quarter):
                children(q)
        here, there = there, here
        nodes *= 2

    paired(stage, 8, lambda j: top_ref[0:8, lanes(j)], lambda j: top_ref[8:16, lanes(j)])
    low = low_lanes(64)
    chain = None
    for level in range(LEVELS):
        value = matrix(stage, 8, level)
        if chain is None:
            found = value
        else:
            wh, wl = split(value)
            vh, vl = split(chain[:, :HALF])
            found = mm(vh, wh) + mm(vl, wh) + mm(vh, wl)
        chain = found
        high = found.astype(bf16).astype(f32)
        top_out_ref[level] = jnp.where(low, swap(high), found - high).astype(bf16)


def down_kernel(
    me_ref, got_ref, near_ref, down_ref, basis_ref, top_ref,
    out_ref,
    values, target, far,
):
    low8 = low_lanes(8)
    low16, _ = half_masks(16)

    def unpack(o, _):
        for s in range(SLOTS):
            at = pl.multiple_of((o * SLOTS + s) * 8, 8)
            values[pl.ds(at, 8), :] = got_ref[o * TILES + s].astype(f32)
        at = pl.multiple_of(o * SLOTS, 8)
        target[pl.ds(at, 8), :] = got_ref[o * TILES + SLOTS + 1].astype(f32)
        return 0

    lax.fori_loop(0, PEERS, unpack, 0, unroll=4)
    landing = jnp.concatenate(
        [target[128 * i : 128 * i + 128, :].T for i in range(SLOTS)], axis=1
    ).astype(bf16)
    for u in range(8):
        chosen = values[pl.ds(u, PEERS * SLOTS, stride=8), :].astype(bf16)
        far[128 * u : 128 * u + 128, :] = mm(landing, chosen)

    def doubled(tile):
        turned = swap(tile)
        both = jnp.concatenate(
            [jnp.where(low8, tile, turned), jnp.where(low8, turned, tile)], axis=0
        )
        return both

    def halves(value):
        high, rest = split(value)
        return jnp.concatenate([high, rest * low16], axis=0)

    me = me_ref[0]
    total = jnp.zeros((2 * NV, HALF), f32)
    for level in range(LEVELS):
        parts = []
        for x in range(2**level, 2 ** (level + 1)):
            tile = got_ref[lax.bitwise_xor(me, x) * TILES + SLOTS].astype(f32)
            if len(parts) < 4:
                parts.append(tile)
            else:
                parts[x % 4] = parts[x % 4] + tile
        tile = parts[0]
        for part in parts[1:]:
            tile = tile + part
        total = total + mmt(halves(doubled(tile)), top_ref[level])
    root = total[:NV] + total[NV:]
    root = halves(jnp.concatenate([root, root], axis=1))

    def leaf_pair(i):
        at = pl.multiple_of(i * 128, 128)
        two = mmt(root, down_ref[pl.ds(at, 128), :])
        f0 = far[pl.ds(2 * i, 8, stride=128), :]
        f1 = far[pl.ds(2 * i + 1, 8, stride=128), :]
        gathered = jnp.concatenate(
            [jnp.where(low8, f0, swap(f1)), jnp.where(low8, swap(f0), f1)], axis=0
        )
        hat = (two[:NV] + two[NV:] + gathered).astype(bf16)
        out_ref[:, pl.ds(at, 128)] = mmt(hat, basis_ref[pl.ds(at, 128), :]) + near_ref[
            :, pl.ds(at, 128)
        ]

    def leaf_block(i, _):
        for k in range(8):
            leaf_pair(8 * i + k)
        return 0

    lax.fori_loop(0, 8, leaf_block, 0)


def vmem():
    return pl.BlockSpec(memory_space=pltpu.VMEM)


def smem():
    return pl.BlockSpec(memory_space=pltpu.SMEM)


def hbm():
    return pl.BlockSpec(memory_space=pl.ANY)


def params():
    return pltpu.CompilerParams(vmem_limit_bytes=VMEM_LIMIT)


def shape(dims, dtype):
    return jax.ShapeDtypeStruct(dims, dtype)


def run_up(me, src, own, dst, x_vecs, basis, edges, top_edges, pairs):
    return pl.pallas_call(
        up_kernel,
        name="up",
        out_shape=(shape((PEERS * TILES, 8, 128), bf16), shape((8, 128), f32)),
        in_specs=[smem(), smem(), smem(), smem(), vmem(), hbm(), hbm(), vmem(), hbm()],
        out_specs=(vmem(), vmem()),
        scratch_shapes=[
            pltpu.VMEM((LEAF_DEV, FLAT), bf16),
            pltpu.VMEM((EDGE_ROWS, FLAT), f32),
            pltpu.VMEM((PAIR_ROWS, FLAT), bf16),
            pltpu.VMEM((1024, 128), f32),
            pltpu.VMEM((64, NV, 128), f32),
            pltpu.VMEM((64, NV, 128), f32),
            pltpu.VMEM((128, 64, 128), bf16),
            pltpu.VMEM((128, 64, 128), bf16),
            pltpu.VMEM((LEAF_DEV, NV, 128), bf16),
            pltpu.VMEM((PEERS * SLOTS, 128), f32),
            pltpu.SMEM((PEERS,), jnp.int32),
            pltpu.SemaphoreType.DMA((3,)),
        ],
        compiler_params=params(),
        cost_estimate=pl.CostEstimate(
            flops=10**9, bytes_accessed=12 * 10**6, transcendentals=0
        ),
    )(me, src, own, dst, x_vecs, basis, edges, top_edges, pairs)


def run_mid(after, xs, xe, near, basis, edges, top):
    return pl.pallas_call(
        mid_kernel,
        name="mid",
        out_shape=(
            shape((NV, LEAF_DEV * LEAF), f32),
            shape((LEAF_DEV * RANK, 128), bf16),
            shape((LEAF_DEV * LEAF, 128), bf16),
            shape((LEVELS, RANK, 128), bf16),
        ),
        in_specs=[vmem(), vmem(), vmem(), hbm(), hbm(), hbm(), vmem()],
        out_specs=(vmem(), vmem(), vmem(), vmem()),
        scratch_shapes=[
            pltpu.VMEM((LEAF_DEV, 3 * FLAT), bf16),
            pltpu.VMEM((LEAF_DEV, FLAT), bf16),
            pltpu.VMEM((EDGE_ROWS, FLAT), f32),
            pltpu.VMEM((1024, 128), f32),
            pltpu.VMEM((1024, 128), f32),
            pltpu.VMEM((64, 64, 128), f32),
            pltpu.VMEM((64, 64, 128), f32),
            pltpu.VMEM((128, 64, 128), bf16),
            pltpu.VMEM((128, 64, 128), bf16),
            pltpu.SemaphoreType.DMA((3,)),
        ],
        compiler_params=params(),
        cost_estimate=pl.CostEstimate(
            flops=10**9, bytes_accessed=14 * 10**6, transcendentals=0
        ),
    )(after, xs, xe, near, basis, edges, top)


def run_down(me, got, near, down, basis, top):
    return pl.pallas_call(
        down_kernel,
        name="down",
        out_shape=shape((NV, LEAF_DEV * LEAF), f32),
        in_specs=[smem(), vmem(), vmem(), vmem(), vmem(), vmem()],
        out_specs=vmem(),
        scratch_shapes=[
            pltpu.VMEM((PEERS * SLOTS * 8, 128), f32),
            pltpu.VMEM((PEERS * SLOTS, 128), f32),
            pltpu.VMEM((8 * LEAF_DEV, 128), f32),
        ],
        compiler_params=params(),
        cost_estimate=pl.CostEstimate(
            flops=10**9, bytes_accessed=8 * 10**6, transcendentals=0
        ),
    )(me, got, near, down, basis, top)


def shards(
    x_vecs,
    leaf_basis,
    near_blocks,
    local_edges,
    top_edges,
    top_couple,
    couple_blocks,
    couple_src,
    couple_owner,
    couple_dst,
):
    ahead = [(i, (i + 1) % PEERS) for i in range(PEERS)]
    back = [(target, source) for source, target in ahead]
    before = lax.ppermute(x_vecs[:, -LEAF:], "leaf", ahead)
    following = lax.ppermute(x_vecs[:, :LEAF], "leaf", back)
    me = lax.axis_index("leaf").astype(jnp.int32).reshape(1)
    outgoing, after = run_up(
        me, couple_src, couple_owner.reshape(PAIR_ROWS), couple_dst, x_vecs, leaf_basis,
        local_edges, top_edges[0], couple_blocks,
    )
    got = lax.all_to_all(
        outgoing.reshape(PEERS, TILES * 8, 128), "leaf", split_axis=0, concat_axis=0, tiled=True
    ).reshape(PEERS * TILES, 8, 128)
    fill = jnp.zeros((NV, LEAF), bf16)
    xs = jnp.concatenate([before, x_vecs, following], axis=1)
    xe = jnp.concatenate([x_vecs, following, fill], axis=1)
    row = jnp.zeros((1, FLAT), f32)
    top = jnp.concatenate([top_edges[0], row, row, top_couple[0], row], axis=0)
    near, down, basis, tops = run_mid(
        after, xs, xe, near_blocks, leaf_basis, local_edges, top
    )
    return run_down(me, got, near, down, basis, tops)


def solution(mesh):
    return jax.shard_map(
        shards,
        mesh=mesh,
        in_specs=(
            P(None, "leaf"),
            P("leaf", None),
            P("leaf", None),
            P("leaf", None),
            P("leaf", None, None),
            P("leaf", None, None),
            P("leaf", None),
            P("leaf"),
            P("leaf", None),
            P("leaf"),
        ),
        out_specs=P(None, "leaf"),
        check_vma=False,
    )
```

```python
import jax
import jax.numpy as jnp
from jax import lax
from jax.experimental import pallas as pl
from jax.experimental.pallas import tpu as pltpu
from jax.sharding import PartitionSpec as P

LEAF = 64
RANK = 64
NV = 16
LEAF_DEV = 128
PEERS = 128
LEVELS = 7
SLOTS = 8
TILES = SLOTS + 2
PAIR_ROWS = 512
EDGE_ROWS = 254
FLAT = 4096
HALF = 64
MIB = 1024 * 1024

LEVEL_BASE = {128: 0, 64: 64, 32: 96, 16: 112, 8: 120, 4: 124, 2: 126}

f32 = jnp.float32
bf16 = jnp.bfloat16


def low_lanes(rows):
    return lax.broadcasted_iota(jnp.int32, (rows, 128), 1) < HALF


def half_masks(rows):
    low = low_lanes(rows).astype(f32)
    return low.astype(bf16), (1.0 - low).astype(bf16)


def swap(value):
    return pltpu.roll(value, HALF, 1)


def join(first, second):
    return jnp.where(low_lanes(first.shape[0]), first, swap(second))


def split(value):
    high = value.astype(bf16)
    return high, (value - high.astype(f32)).astype(bf16)


def mm(left, right):
    return jnp.dot(left, right, preferred_element_type=f32)


def mmt(left, right):
    return lax.dot_general(left, right, (((1,), (1,)), ((), ())), preferred_element_type=f32)


def paired(stage, group, load_first, load_second):
    low = low_lanes(group)
    for j in range(32):
        first = load_first(j)
        second = load_second(j)
        stage[pl.ds(2 * j * group, group), :] = jnp.where(low, first, swap(second))
        stage[pl.ds((2 * j + 1) * group, group), :] = jnp.where(low, swap(first), second)


def matrix(stage, group, index):
    return stage[pl.ds(index, 64, stride=group), :]


def lanes(j, start=0):
    return pl.ds(start + j * 128, 128)


def relayout_edges(edges, stage, highs, lows):
    def keep(index, place):
        high, low = split(matrix(stage, 8, index))
        highs[place] = high
        lows[place] = low

    def group(g, _):
        first = jnp.where(
            g < 8, 8 * g, jnp.where(g < 12, 64 + 8 * g, jnp.where(g < 14, 96 + 8 * g, 224))
        )
        gap = jnp.where(g < 8, 64, jnp.where(g < 12, 32, jnp.where(g < 14, 16, 8)))
        first = pl.multiple_of(first, 8)
        second = pl.multiple_of(first + gap, 8)
        paired(
            stage,
            8,
            lambda j: edges[pl.ds(first, 8), lanes(j)],
            lambda j: edges[pl.ds(second, 8), lanes(j)],
        )
        for i in range(8):
            keep(i, 8 * g + i)
        return 0

    lax.fori_loop(0, 15, group, 0)
    paired(
        stage,
        8,
        lambda j: edges[240:248, lanes(j)],
        lambda j: pltpu.roll(edges[240:248, lanes(j)], 4, 0),
    )
    for i in range(4):
        keep(i, 120 + i)
    rows = lax.broadcasted_iota(jnp.int32, (8, 128), 0)

    def last_second(j):
        tile = edges[246:254, lanes(j)]
        return jnp.where(rows < 6, pltpu.roll(tile, 6, 0), pltpu.roll(tile, 7, 0))

    paired(stage, 8, lambda j: edges[246:254, lanes(j)], last_second)
    keep(2, 124)
    keep(3, 125)
    keep(6, 126)


def up_kernel(
    me_ref, src_ref, own_ref, dst_ref, x_ref, basis_hbm, edges_hbm, top_ref, pairs_hbm,
    out_ref, done_ref,
    basis, edges, pairs, stage, stage_two, vec_a, vec_b, highs, lows, table, rows_at, count, sems,
):
    copies = [
        pltpu.make_async_copy(basis_hbm, basis, sems.at[0]),
        pltpu.make_async_copy(edges_hbm, edges, sems.at[1]),
        pltpu.make_async_copy(pairs_hbm, pairs, sems.at[2]),
    ]
    for copy in copies:
        copy.start()
    low16, high16 = half_masks(16)
    low = low_lanes(16)

    def clear(i, _):
        out_ref[pl.ds(i * 16, 16)] = jnp.zeros((16, 8, 128), bf16)
        return 0

    lax.fori_loop(0, PEERS * TILES // 16, clear, 0)
    rows_at[...] = jnp.zeros_like(rows_at)

    def clear_count(i, _):
        count[i] = 0
        return 0

    lax.fori_loop(0, PEERS, clear_count, 0)

    copies[0].wait()

    def leaf_group(g, _):
        first = pl.multiple_of(16 * g, 16)
        second = pl.multiple_of(64 + 16 * g, 16)
        paired(
            stage,
            16,
            lambda j: basis[pl.ds(first, 16), lanes(j)].astype(f32),
            lambda j: basis[pl.ds(second, 16), lanes(j)].astype(f32),
        )
        for i in range(0, 16, 2):
            weight = jnp.concatenate([matrix(stage, 16, i), matrix(stage, 16, i + 1)], axis=0)
            at = pl.multiple_of(g * 1024 + i * 64, 128)
            left = x_ref[:, pl.ds(at, 128)]
            right = x_ref[:, pl.ds(pl.multiple_of(at + FLAT, 128), 128)]
            stacked = jnp.concatenate(
                [left * low16, right * low16, left * high16, right * high16], axis=0
            )
            found = mm(stacked, weight.astype(bf16))
            for k in range(2):
                pair = jnp.where(low, found[32 * k : 32 * k + 16], found[32 * k + 16 : 32 * k + 32])
                turned = swap(pair)
                t = 16 * g + i + k
                vec_a[t] = pair
                table[t] = jnp.where(low, pair, turned).astype(bf16)
                table[t + 64] = jnp.where(low, turned, pair).astype(bf16)
        return 0

    lax.fori_loop(0, 4, leaf_group, 0)

    copies[1].wait()
    relayout_edges(edges, stage, highs, lows)

    here, there = vec_a, vec_b
    nodes = LEAF_DEV
    while nodes > 2:
        base = LEVEL_BASE[nodes]

        def parent(q, here=here, there=there, base=base):
            p0 = here[2 * q]
            p1 = here[2 * q + 1]
            both = jnp.concatenate(
                [jnp.where(low, p0, swap(p1)), jnp.where(low, swap(p0), p1)], axis=0
            )
            vh, vl = split(both)
            wh = highs[pl.ds(base + 2 * q, 2)].reshape(128, 128)
            wl = lows[pl.ds(base + 2 * q, 2)].reshape(128, 128)
            two = mm(jnp.concatenate([vh, vl], axis=0), wh)
            found = two[:32] + two[32:] + mm(vh, wl)
            there[q] = jnp.where(low, found[:16], found[16:])

        quarter = nodes // 4
        if quarter > 8:

            def block(i, _, parent=parent):
                for k in range(8):
                    parent(8 * i + k)
                return 0

            lax.fori_loop(0, quarter // 8, block, 0)
        else:
            for q in range(quarter):
                parent(q)
        here, there = there, here
        nodes //= 2
    last = here[0]
    both = jnp.concatenate([last, swap(last)], axis=0)[:, :HALF]
    vh, vl = split(both)
    wh = highs[126]
    two = mm(jnp.concatenate([vh, vl], axis=0), wh)
    found = two[:32] + two[32:] + mm(vh, lows[126])
    current = found[:16] + swap(found[16:])

    for level in range(LEVELS - 1):
        tile = top_ref[32 * level : 32 * level + 32, :]
        stage[pl.ds(64 * level, 32, stride=2), :] = tile
        stage[pl.ds(64 * level + 1, 32, stride=2), :] = swap(tile)
    me = me_ref[0]
    for level in range(LEVELS):
        tile = join(current[0:8], current[8:16]).astype(bf16)
        for x in range(2**level, 2 ** (level + 1)):
            out_ref[lax.bitwise_xor(me, x) * TILES + SLOTS] = tile
        if level < LEVELS - 1:
            wh, wl = split(stage[64 * level : 64 * level + 64, :])
            vh, vl = split(current[:, :HALF])
            two = mm(jnp.concatenate([vh, vl], axis=0), wh)
            current = two[:16] + two[16:] + mm(vh, wl)

    copies[2].wait()
    lane_ids = lax.broadcasted_iota(jnp.int32, (1, 128), 1)

    def pair_layout(g, to):
        first = pl.multiple_of(32 * g, 16)
        second = pl.multiple_of(32 * g + 16, 16)
        paired(
            to,
            16,
            lambda j: pairs[pl.ds(first, 16), lanes(j)].astype(f32),
            lambda j: pairs[pl.ds(second, 16), lanes(j)].astype(f32),
        )

    def pair_products(g, at):
        for i in range(16):
            weight = matrix(at, 16, i).astype(bf16)
            listed = [32 * g + i, 32 * g + 16 + i]
            stacked = jnp.concatenate(
                [table[src_ref[listed[0]]] * low16, table[src_ref[listed[1]]] * high16], axis=0
            )
            found = mmt(stacked, weight)
            for k in range(2):
                owner = own_ref[listed[k]]
                rank = count[owner]
                count[owner] = rank + 1
                tile = jnp.concatenate(
                    [found[16 * k : 16 * k + 8], found[16 * k + 8 : 16 * k + 16]], axis=1
                )
                out_ref[owner * TILES + rank] = tile.astype(bf16)
                rows_at[pl.ds(owner * SLOTS + rank, 1), :] = jnp.where(
                    lane_ids == dst_ref[listed[k]], 1.0, 0.0
                )

    groups = PAIR_ROWS // 32
    pair_layout(0, stage)

    def pair_step(h, _):
        pair_layout(2 * h + 1, stage_two)
        pair_products(2 * h, stage)
        pair_layout(jnp.minimum(2 * h + 2, groups - 1), stage)
        pair_products(2 * h + 1, stage_two)
        return 0

    lax.fori_loop(0, groups // 2, pair_step, 0)

    def place_rows(o, _):
        out_ref[o * TILES + SLOTS + 1] = rows_at[
            pl.ds(pl.multiple_of(o * SLOTS, 8), 8), :
        ].astype(bf16)
        return 0

    lax.fori_loop(0, PEERS, place_rows, 0, unroll=8)
    done_ref[...] = current[0:8]


def mid_kernel(
    after_ref, xs_ref, xe_ref, near_hbm, basis_hbm, edges_hbm, top_ref, couple_ref,
    near_ref, down_ref, basis_ref, top_out_ref,
    near, basis, edges, stage, stage_two, vec_a, vec_b, highs, lows, sems,
):
    copies = [
        pltpu.make_async_copy(near_hbm, near, sems.at[0]),
        pltpu.make_async_copy(basis_hbm, basis, sems.at[1]),
        pltpu.make_async_copy(edges_hbm, edges, sems.at[2]),
    ]
    for copy in copies:
        copy.start()
    low16, _ = half_masks(16)
    low64, high64 = half_masks(64)

    copies[0].wait()

    def near_group(g, _):
        first = pl.multiple_of(16 * g, 16)
        rows = pl.ds(first, 16)
        paired(
            stage,
            16,
            lambda j: near[rows, lanes(j)].astype(f32),
            lambda j: near[rows, lanes(j, FLAT)].astype(f32),
        )
        for j in range(32):
            tile = near[rows, lanes(j, 2 * FLAT)].astype(f32)
            stage_two[pl.ds(32 * j, 16), :] = tile
            stage_two[pl.ds(32 * j + 16, 16), :] = swap(tile)
        for i in range(0, 16, 2):
            at = pl.multiple_of(g * 1024 + i * 64, 128)
            after = pl.multiple_of(at + 128, 128)
            found = []
            for k, ref in enumerate((xs_ref, xe_ref)):
                weight = jnp.concatenate(
                    [matrix(stage, 16, i + k), matrix(stage_two, 16, i + k)], axis=1
                ).astype(bf16)
                vec = jnp.concatenate(
                    [ref[:, pl.ds(at, 128)], ref[:, pl.ds(after, 128)] * low16], axis=1
                )
                found.append(mmt(vec, weight))
            near_ref[:, pl.ds(at, 128)] = jnp.concatenate(found, axis=1)
        return 0

    lax.fori_loop(0, 8, near_group, 0)

    copies[1].wait()
    wide = low_lanes(64)
    even = (lax.broadcasted_iota(jnp.int32, (16, 128), 0) % 2) == 0

    def basis_group(g, _):
        rows = pl.ds(pl.multiple_of(16 * g, 16), 16)
        for j in range(32):
            tile = basis[rows, lanes(j)].astype(f32)
            turned = swap(tile)
            stage[pl.ds(32 * j, 16), :] = jnp.where(even, tile, turned)
            stage[pl.ds(32 * j + 16, 16), :] = jnp.where(even, turned, tile)
        for i in range(0, 16, 2):
            at = pl.multiple_of(g * 512 + i * 32, 64)
            basis_ref[pl.ds(at, 64), :] = jnp.where(
                wide, matrix(stage, 16, i), matrix(stage, 16, i + 1)
            ).astype(bf16)
        return 0

    lax.fori_loop(0, 8, basis_group, 0)

    copies[2].wait()
    relayout_edges(edges, stage, highs, lows)
    vec_a[0] = highs[126].astype(f32) + lows[126].astype(f32)
    here, there = vec_a, vec_b
    nodes = 4
    while nodes <= LEAF_DEV:
        base = LEVEL_BASE[nodes]

        def children(q, here=here, there=there, base=base, final=nodes == LEAF_DEV):
            ph, plow = split(here[q])
            rh = jnp.concatenate([ph * low64, ph * high64], axis=0)
            rl = jnp.concatenate([plow * low64, plow * high64], axis=0)
            wh = highs[pl.ds(base + 2 * q, 2)].reshape(128, 128)
            wl = lows[pl.ds(base + 2 * q, 2)].reshape(128, 128)
            found = mm(wh, rh) + mm(wl, rh) + mm(wh, rl)
            if not final:
                there[2 * q] = found[:64]
                there[2 * q + 1] = found[64:]
            else:
                at = pl.multiple_of(q * 128, 128)
                down_ref[pl.ds(at, 128), :] = found.astype(bf16)

        quarter = nodes // 4
        if quarter > 4:

            def block(i, _, children=children):
                for k in range(4):
                    children(4 * i + k)
                return 0

            lax.fori_loop(0, quarter // 4, block, 0)
        else:
            for q in range(quarter):
                children(q)
        here, there = there, here
        nodes *= 2

    low = low_lanes(64)
    low32 = low_lanes(32)
    for level in range(LEVELS):
        second = couple_ref[32 * level : 32 * level + 32, :]
        first = top_ref[32 * level : 32 * level + 32, :] if level < LEVELS - 1 else second
        stage[pl.ds(64 * level, 32, stride=2), :] = jnp.where(low32, first, swap(second))
        stage[pl.ds(64 * level + 1, 32, stride=2), :] = jnp.where(low32, swap(first), second)
    chain = None
    for level in range(LEVELS):
        value = stage[64 * level : 64 * level + 64, :]
        if chain is None:
            found = value
        else:
            wh, wl = split(value)
            vh, vl = split(chain[:, :HALF])
            found = mm(vh, wh) + mm(vl, wh) + mm(vh, wl)
        chain = found
        high = found.astype(bf16).astype(f32)
        top_out_ref[level] = jnp.where(low, swap(high), found - high).astype(bf16)


def down_kernel(
    me_ref, got_hbm, near_hbm, down_hbm, basis_hbm, top_ref,
    out_ref,
    got, near, down, basis, values, target, far, hats, sems,
):
    copies = [
        pltpu.make_async_copy(got_hbm, got, sems.at[0]),
        pltpu.make_async_copy(down_hbm, down, sems.at[1]),
        pltpu.make_async_copy(basis_hbm, basis, sems.at[2]),
        pltpu.make_async_copy(near_hbm, near, sems.at[3]),
    ]
    for copy in copies:
        copy.start()
    low8 = low_lanes(8)
    low16, high16 = half_masks(16)
    copies[0].wait()

    def unpack(o, _):
        for s in range(SLOTS):
            at = pl.multiple_of((o * SLOTS + s) * 8, 8)
            values[pl.ds(at, 8), :] = got[o * TILES + s].astype(f32)
        at = pl.multiple_of(o * SLOTS, 8)
        target[pl.ds(at, 8), :] = got[o * TILES + SLOTS + 1].astype(f32)
        return 0

    lax.fori_loop(0, PEERS, unpack, 0, unroll=4)
    landing = jnp.concatenate(
        [target[128 * i : 128 * i + 128, :].T for i in range(SLOTS)], axis=1
    ).astype(bf16)
    for u in range(0, 8, 2):
        chosen = jnp.concatenate(
            [values[pl.ds(u + k, PEERS * SLOTS, stride=8), :] for k in range(2)], axis=1
        ).astype(bf16)
        found = mm(landing, chosen)
        far[128 * u : 128 * u + 128, :] = found[:, :128]
        far[128 * u + 128 : 128 * u + 256, :] = found[:, 128:]

    def doubled(tile):
        turned = swap(tile)
        return jnp.concatenate(
            [jnp.where(low8, tile, turned), jnp.where(low8, turned, tile)], axis=0
        )

    me = me_ref[0]
    total = jnp.zeros((2 * NV, HALF), f32)
    for level in range(LEVELS):
        parts = []
        for x in range(2**level, 2 ** (level + 1)):
            tile = got[lax.bitwise_xor(me, x) * TILES + SLOTS].astype(f32)
            if len(parts) < 4:
                parts.append(tile)
            else:
                parts[x % 4] = parts[x % 4] + tile
        tile = parts[0]
        for part in parts[1:]:
            tile = tile + part
        high, rest = split(doubled(tile))
        total = total + mmt(jnp.concatenate([high, rest * low16], axis=0), top_ref[level])
    root = total[:NV] + total[NV:]
    high, rest = split(jnp.concatenate([root, root], axis=1))
    root = jnp.concatenate([high * low16, high * high16, rest * low16, rest * high16], axis=0)

    copies[1].wait()

    def hat_block(c, _):
        at = pl.multiple_of(c * 512, 512)
        found = mmt(root, down[pl.ds(at, 512), :])
        for half in range(2):
            block = found[16 * half : 16 * half + 16] + found[32 + 16 * half : 48 + 16 * half]
            for k in range(4):
                leaf = 64 * half + 8 * c + 2 * k
                f0 = far[pl.ds(leaf, 8, stride=128), :]
                f1 = far[pl.ds(leaf + 1, 8, stride=128), :]
                gathered = jnp.concatenate(
                    [jnp.where(low8, f0, swap(f1)), jnp.where(low8, swap(f0), f1)], axis=0
                )
                to = pl.multiple_of(half * FLAT + c * 512 + k * 128, 128)
                hats[:, pl.ds(to, 128)] = (block[:, 128 * k : 128 * k + 128] + gathered).astype(
                    bf16
                )
        return 0

    lax.fori_loop(0, 8, hat_block, 0)
    copies[2].wait()
    copies[3].wait()

    def leaf_block(i, _):
        for k in range(8):
            at = pl.multiple_of(i * 1024 + k * 128, 128)
            hat = hats[:, pl.ds(at, 128)]
            weight = basis[pl.ds(pl.multiple_of(i * 512 + k * 64, 64), 64), :]
            found = mmt(jnp.concatenate([hat * low16, hat * high16], axis=0), weight)
            out_ref[:, pl.ds(at, 128)] = (
                jnp.concatenate([found[:NV], found[NV:]], axis=1) + near[:, pl.ds(at, 128)]
            )
        return 0

    lax.fori_loop(0, 8, leaf_block, 0)


def vmem():
    return pl.BlockSpec(memory_space=pltpu.VMEM)


def smem():
    return pl.BlockSpec(memory_space=pltpu.SMEM)


def hbm():
    return pl.BlockSpec(memory_space=pl.ANY)


def params(mib):
    return pltpu.CompilerParams(vmem_limit_bytes=mib * MIB)


def shape(dims, dtype):
    return jax.ShapeDtypeStruct(dims, dtype)


def run_up(me, src, own, dst, x_vecs, basis, edges, top_edges, pairs):
    return pl.pallas_call(
        up_kernel,
        name="up",
        out_shape=(shape((PEERS * TILES, 8, 128), bf16), shape((8, 128), f32)),
        in_specs=[smem(), smem(), smem(), smem(), vmem(), hbm(), hbm(), vmem(), hbm()],
        out_specs=(vmem(), vmem()),
        scratch_shapes=[
            pltpu.VMEM((LEAF_DEV, FLAT), bf16),
            pltpu.VMEM((EDGE_ROWS, FLAT), f32),
            pltpu.VMEM((PAIR_ROWS, FLAT), bf16),
            pltpu.VMEM((1024, 128), f32),
            pltpu.VMEM((1024, 128), f32),
            pltpu.VMEM((64, NV, 128), f32),
            pltpu.VMEM((64, NV, 128), f32),
            pltpu.VMEM((128, 64, 128), bf16),
            pltpu.VMEM((128, 64, 128), bf16),
            pltpu.VMEM((LEAF_DEV, NV, 128), bf16),
            pltpu.VMEM((PEERS * SLOTS, 128), f32),
            pltpu.SMEM((PEERS,), jnp.int32),
            pltpu.SemaphoreType.DMA((3,)),
        ],
        compiler_params=params(60),
        cost_estimate=pl.CostEstimate(
            flops=10**9, bytes_accessed=12 * 10**6, transcendentals=0
        ),
    )(me, src, own, dst, x_vecs, basis, edges, top_edges, pairs)


def run_mid(after, xs, xe, near, basis, edges, top, couple):
    return pl.pallas_call(
        mid_kernel,
        name="mid",
        out_shape=(
            shape((NV, LEAF_DEV * LEAF), f32),
            shape((LEAF_DEV * RANK // 2, 128), bf16),
            shape((LEAF_DEV * LEAF // 2, 128), bf16),
            shape((LEVELS, RANK, 128), bf16),
        ),
        in_specs=[vmem(), vmem(), vmem(), hbm(), hbm(), hbm(), vmem(), vmem()],
        out_specs=(vmem(), vmem(), vmem(), vmem()),
        scratch_shapes=[
            pltpu.VMEM((LEAF_DEV, 3 * FLAT), bf16),
            pltpu.VMEM((LEAF_DEV, FLAT), bf16),
            pltpu.VMEM((EDGE_ROWS, FLAT), f32),
            pltpu.VMEM((1024, 128), f32),
            pltpu.VMEM((1024, 128), f32),
            pltpu.VMEM((64, 64, 128), f32),
            pltpu.VMEM((64, 64, 128), f32),
            pltpu.VMEM((128, 64, 128), bf16),
            pltpu.VMEM((128, 64, 128), bf16),
            pltpu.SemaphoreType.DMA((3,)),
        ],
        compiler_params=params(24),
        cost_estimate=pl.CostEstimate(
            flops=10**9, bytes_accessed=14 * 10**6, transcendentals=0
        ),
    )(after, xs, xe, near, basis, edges, top, couple)


def run_down(me, got, near, down, basis, top):
    return pl.pallas_call(
        down_kernel,
        name="down",
        out_shape=shape((NV, LEAF_DEV * LEAF), f32),
        in_specs=[smem(), hbm(), hbm(), hbm(), hbm(), vmem()],
        out_specs=vmem(),
        scratch_shapes=[
            pltpu.VMEM((PEERS * TILES, 8, 128), bf16),
            pltpu.VMEM((NV, LEAF_DEV * LEAF), f32),
            pltpu.VMEM((LEAF_DEV * RANK // 2, 128), bf16),
            pltpu.VMEM((LEAF_DEV * LEAF // 2, 128), bf16),
            pltpu.VMEM((PEERS * SLOTS * 8, 128), f32),
            pltpu.VMEM((PEERS * SLOTS, 128), f32),
            pltpu.VMEM((8 * LEAF_DEV, 128), f32),
            pltpu.VMEM((NV, LEAF_DEV * LEAF), bf16),
            pltpu.SemaphoreType.DMA((4,)),
        ],
        compiler_params=params(16),
        cost_estimate=pl.CostEstimate(
            flops=10**9, bytes_accessed=8 * 10**6, transcendentals=0
        ),
    )(me, got, near, down, basis, top)


def shards(
    x_vecs,
    leaf_basis,
    near_blocks,
    local_edges,
    top_edges,
    top_couple,
    couple_blocks,
    couple_src,
    couple_owner,
    couple_dst,
):
    ahead = [(i, (i + 1) % PEERS) for i in range(PEERS)]
    back = [(target, source) for source, target in ahead]
    before = lax.ppermute(x_vecs[:, -LEAF:], "leaf", ahead)
    following = lax.ppermute(x_vecs[:, :LEAF], "leaf", back)
    top_flat = top_edges.reshape((LEVELS - 1) * 32, 128)
    me = lax.axis_index("leaf").astype(jnp.int32).reshape(1)
    outgoing, after = run_up(
        me, couple_src, couple_owner.reshape(PAIR_ROWS), couple_dst, x_vecs, leaf_basis,
        local_edges, top_flat, couple_blocks,
    )
    outgoing, before, following = lax.optimization_barrier((outgoing, before, following))
    got = lax.all_to_all(
        outgoing.reshape(PEERS, TILES * 8, 128), "leaf", split_axis=0, concat_axis=0, tiled=True
    ).reshape(PEERS * TILES, 8, 128)
    fill = jnp.zeros((NV, LEAF), bf16)
    xs = jnp.concatenate([before, x_vecs, following], axis=1)
    xe = jnp.concatenate([x_vecs, following, fill], axis=1)
    near, down, basis, tops = run_mid(
        after, xs, xe, near_blocks, leaf_basis, local_edges, top_flat,
        top_couple.reshape(LEVELS * 32, 128),
    )
    return run_down(me, got, near, down, basis, tops)


def solution(mesh):
    return jax.shard_map(
        shards,
        mesh=mesh,
        in_specs=(
            P(None, "leaf"),
            P("leaf", None),
            P("leaf", None),
            P("leaf", None),
            P("leaf", None, None),
            P("leaf", None, None),
            P("leaf", None),
            P("leaf"),
            P("leaf", None),
            P("leaf"),
        ),
        out_specs=P(None, "leaf"),
        check_vma=False,
    )
```

```python
import jax
import jax.numpy as jnp
from jax import lax
from jax.experimental import pallas as pl
from jax.experimental.pallas import tpu as pltpu
from jax.sharding import PartitionSpec as P

LEAF = 64
RANK = 64
NV = 16
LEAF_DEV = 128
PEERS = 128
LEVELS = 7
SLOTS = 8
TILES = SLOTS + 2
PAIR_ROWS = 512
EDGE_ROWS = 254
FLAT = 4096
HALF = 64
MIB = 1024 * 1024

LEVEL_BASE = {128: 0, 64: 64, 32: 96, 16: 112, 8: 120, 4: 124, 2: 126}

f32 = jnp.float32
bf16 = jnp.bfloat16


def low_lanes(rows):
    return lax.broadcasted_iota(jnp.int32, (rows, 128), 1) < HALF


def half_masks(rows):
    low = low_lanes(rows).astype(f32)
    return low.astype(bf16), (1.0 - low).astype(bf16)


def swap(value):
    return pltpu.roll(value, HALF, 1)


def join(first, second):
    return jnp.where(low_lanes(first.shape[0]), first, swap(second))


def split(value):
    high = value.astype(bf16)
    return high, (value - high.astype(f32)).astype(bf16)


def mm(left, right):
    return jnp.dot(left, right, preferred_element_type=f32)


def mmt(left, right):
    return lax.dot_general(left, right, (((1,), (1,)), ((), ())), preferred_element_type=f32)


def paired(stage, group, load_first, load_second):
    low = low_lanes(group)
    for j in range(32):
        first = load_first(j)
        second = load_second(j)
        stage[pl.ds(2 * j * group, group), :] = jnp.where(low, first, swap(second))
        stage[pl.ds((2 * j + 1) * group, group), :] = jnp.where(low, swap(first), second)


def matrix(stage, group, index):
    return stage[pl.ds(index, 64, stride=group), :]


def lanes(j, start=0):
    return pl.ds(start + j * 128, 128)


def relayout_edges(edges, stage, stage_two, highs, lows):
    def keep(at, index, place):
        high, low = split(matrix(at, 8, index))
        highs[place] = high
        lows[place] = low

    def layout(g, to):
        first = jnp.where(
            g < 8, 8 * g, jnp.where(g < 12, 64 + 8 * g, jnp.where(g < 14, 96 + 8 * g, 224))
        )
        gap = jnp.where(g < 8, 64, jnp.where(g < 12, 32, jnp.where(g < 14, 16, 8)))
        first = pl.multiple_of(first, 8)
        second = pl.multiple_of(first + gap, 8)
        paired(
            to,
            8,
            lambda j: edges[pl.ds(first, 8), lanes(j)],
            lambda j: edges[pl.ds(second, 8), lanes(j)],
        )

    def step(h, _):
        odd = jnp.minimum(2 * h + 1, 14)
        layout(2 * h, stage)
        layout(odd, stage_two)
        for i in range(8):
            keep(stage, i, 16 * h + i)
        for i in range(8):
            keep(stage_two, i, 8 * odd + i)
        return 0

    lax.fori_loop(0, 8, step, 0)
    paired(
        stage,
        8,
        lambda j: edges[240:248, lanes(j)],
        lambda j: pltpu.roll(edges[240:248, lanes(j)], 4, 0),
    )
    rows = lax.broadcasted_iota(jnp.int32, (8, 128), 0)

    def last_second(j):
        tile = edges[246:254, lanes(j)]
        return jnp.where(rows < 6, pltpu.roll(tile, 6, 0), pltpu.roll(tile, 7, 0))

    paired(stage_two, 8, lambda j: edges[246:254, lanes(j)], last_second)
    for i in range(4):
        keep(stage, i, 120 + i)
    keep(stage_two, 2, 124)
    keep(stage_two, 3, 125)
    keep(stage_two, 6, 126)


def up_kernel(
    x_ref, top_ref, src_hbm, own_hbm, dst_hbm, basis_hbm, edges_hbm, pairs_hbm,
    out_ref, done_ref,
    src_ref, own_ref, dst_ref, basis, edges, pairs, stage, stage_two, tops, vec_a, vec_b,
    highs, lows, table, rows_at, count, sems,
):
    basis_copy = pltpu.make_async_copy(basis_hbm, basis, sems.at[0])
    edges_copy = pltpu.make_async_copy(edges_hbm, edges, sems.at[1])
    pairs_copy = pltpu.make_async_copy(pairs_hbm, pairs, sems.at[2])
    lists = [
        pltpu.make_async_copy(src_hbm, src_ref, sems.at[3]),
        pltpu.make_async_copy(own_hbm, own_ref, sems.at[4]),
        pltpu.make_async_copy(dst_hbm, dst_ref, sems.at[5]),
    ]
    basis_copy.start()
    edges_copy.start()
    for copy in lists:
        copy.start()
    low16, high16 = half_masks(16)
    low = low_lanes(16)

    def clear(i, _):
        out_ref[pl.ds(i * 32, 32)] = jnp.zeros((32, 8, 128), bf16)
        return 0

    lax.fori_loop(0, PEERS * TILES // 32, clear, 0)
    rows_at[...] = jnp.zeros_like(rows_at)

    def clear_count(i, _):
        for k in range(16):
            count[16 * i + k] = 0
        return 0

    lax.fori_loop(0, PEERS // 16, clear_count, 0)
    for level in range(LEVELS - 1):
        tile = top_ref[32 * level : 32 * level + 32, :]
        tops[pl.ds(64 * level, 32, stride=2), :] = tile
        tops[pl.ds(64 * level + 1, 32, stride=2), :] = swap(tile)

    basis_copy.wait()
    pairs_copy.start()

    def leaf_layout(g, to):
        first = pl.multiple_of(16 * g, 16)
        second = pl.multiple_of(64 + 16 * g, 16)
        paired(
            to,
            16,
            lambda j: basis[pl.ds(first, 16), lanes(j)].astype(f32),
            lambda j: basis[pl.ds(second, 16), lanes(j)].astype(f32),
        )

    def leaf_products(g, at_stage):
        for i in range(0, 16, 2):
            weight = jnp.concatenate([matrix(at_stage, 16, i), matrix(at_stage, 16, i + 1)], axis=0)
            at = pl.multiple_of(g * 1024 + i * 64, 128)
            left = x_ref[:, pl.ds(at, 128)]
            right = x_ref[:, pl.ds(pl.multiple_of(at + FLAT, 128), 128)]
            stacked = jnp.concatenate(
                [left * low16, right * low16, left * high16, right * high16], axis=0
            )
            found = mm(stacked, weight.astype(bf16))
            for k in range(2):
                pair = jnp.where(low, found[32 * k : 32 * k + 16], found[32 * k + 16 : 32 * k + 32])
                turned = swap(pair)
                t = 16 * g + i + k
                vec_a[t] = pair
                table[t] = jnp.where(low, pair, turned).astype(bf16)
                table[t + 64] = jnp.where(low, turned, pair).astype(bf16)

    def leaf_step(h, _):
        leaf_layout(2 * h, stage)
        leaf_layout(2 * h + 1, stage_two)
        leaf_products(2 * h, stage)
        leaf_products(2 * h + 1, stage_two)
        return 0

    lax.fori_loop(0, 2, leaf_step, 0)

    edges_copy.wait()
    relayout_edges(edges, stage, stage_two, highs, lows)

    def parents(nodes, first, amount):
        up = nodes in (128, 32, 8)
        here, there = (vec_a, vec_b) if up else (vec_b, vec_a)
        base = LEVEL_BASE[nodes]
        for k in range(amount):
            q = first + k
            p0 = here[2 * q]
            p1 = here[2 * q + 1]
            both = jnp.concatenate(
                [jnp.where(low, p0, swap(p1)), jnp.where(low, swap(p0), p1)], axis=0
            )
            vh, vl = split(both)
            wh = highs[pl.ds(base + 2 * q, 2)].reshape(128, 128)
            wl = lows[pl.ds(base + 2 * q, 2)].reshape(128, 128)
            two = mm(jnp.concatenate([vh, vl], axis=0), wh)
            found = two[:32] + two[32:] + mm(vh, wl)
            there[q] = jnp.where(low, found[:16], found[16:])

    def root():
        last = vec_a[0]
        both = jnp.concatenate([last, swap(last)], axis=0)[:, :HALF]
        vh, vl = split(both)
        two = mm(jnp.concatenate([vh, vl], axis=0), highs[126])
        found = two[:32] + two[32:] + mm(vh, lows[126])
        return found[:16] + swap(found[16:])

    def carried(current, level):
        wh, wl = split(tops[64 * level : 64 * level + 64, :])
        vh, vl = split(current[:, :HALF])
        two = mm(jnp.concatenate([vh, vl], axis=0), wh)
        return two[:16] + two[16:] + mm(vh, wl)

    me = lax.axis_index("leaf").astype(jnp.int32)

    def send(current, level):
        tile = join(current[0:8], current[8:16]).astype(bf16)
        for x in range(2**level, 2 ** (level + 1)):
            out_ref[lax.bitwise_xor(me, x) * TILES + SLOTS] = tile

    for copy in lists:
        copy.wait()
    pairs_copy.wait()
    lane_ids = lax.broadcasted_iota(jnp.int32, (1, 128), 1)

    def pair_layout(g, to):
        first = pl.multiple_of(32 * g, 16)
        second = pl.multiple_of(32 * g + 16, 16)
        paired(
            to,
            16,
            lambda j: pairs[pl.ds(first, 16), lanes(j)].astype(f32),
            lambda j: pairs[pl.ds(second, 16), lanes(j)].astype(f32),
        )

    def pair_products(g, at):
        zero = jnp.zeros((32, 128), bf16)
        for i in range(0, 16, 2):
            weight = jnp.concatenate(
                [matrix(at, 16, i), matrix(at, 16, i + 1)], axis=1
            ).astype(bf16)
            listed = [32 * g + i, 32 * g + 16 + i, 32 * g + i + 1, 32 * g + 17 + i]
            sources = [table[src_ref[r]] for r in listed]
            first = jnp.concatenate([sources[0] * low16, sources[1] * high16], axis=0)
            second = jnp.concatenate([sources[2] * low16, sources[3] * high16], axis=0)
            stacked = jnp.concatenate(
                [
                    jnp.concatenate([first, zero], axis=1),
                    jnp.concatenate([zero, second], axis=1),
                ],
                axis=0,
            )
            found = mmt(stacked, weight)
            for k in range(4):
                owner = own_ref[listed[k]]
                rank = count[owner]
                count[owner] = rank + 1
                tile = jnp.concatenate(
                    [found[16 * k : 16 * k + 8], found[16 * k + 8 : 16 * k + 16]], axis=1
                )
                out_ref[owner * TILES + rank] = tile.astype(bf16)
                rows_at[pl.ds(owner * SLOTS + rank, 1), :] = jnp.where(
                    lane_ids == dst_ref[listed[k]], 1.0, 0.0
                )

    groups = PAIR_ROWS // 32
    pair_layout(0, stage)

    def pair_step(h):
        pair_layout(2 * h + 1, stage_two)
        pair_products(2 * h, stage)
        pair_layout(jnp.minimum(2 * h + 2, groups - 1), stage)
        pair_products(2 * h + 1, stage_two)

    def first_steps(h, _):
        parents(128, 8 * h, 8)
        pair_step(h)
        return 0

    lax.fori_loop(0, 4, first_steps, 0)
    parents(64, 0, 16)
    pair_step(4)
    parents(32, 0, 8)
    parents(16, 0, 4)
    pair_step(5)
    parents(8, 0, 2)
    parents(4, 0, 1)
    current = root()
    send(current, 0)
    current = carried(current, 0)
    pair_step(6)
    for level in range(1, LEVELS):
        send(current, level)
        if level < LEVELS - 1:
            current = carried(current, level)
    pair_step(7)

    def place_rows(o, _):
        out_ref[o * TILES + SLOTS + 1] = rows_at[
            pl.ds(pl.multiple_of(o * SLOTS, 8), 8), :
        ].astype(bf16)
        return 0

    lax.fori_loop(0, PEERS, place_rows, 0, unroll=16)
    done_ref[...] = current[0:8]


def mid_kernel(
    after_ref, xs_ref, xe_ref, near_hbm, basis_hbm, edges_hbm, top_ref, couple_ref,
    near_ref, down_ref, basis_ref, top_out_ref,
    near, basis, edges, stage, stage_two, vec_a, vec_b, highs, lows, sems,
):
    copies = [
        pltpu.make_async_copy(near_hbm, near, sems.at[0]),
        pltpu.make_async_copy(basis_hbm, basis, sems.at[1]),
        pltpu.make_async_copy(edges_hbm, edges, sems.at[2]),
    ]
    for copy in copies:
        copy.start()
    low16, _ = half_masks(16)
    low64, high64 = half_masks(64)

    copies[0].wait()

    def near_group(g, _):
        first = pl.multiple_of(16 * g, 16)
        rows = pl.ds(first, 16)
        paired(
            stage,
            16,
            lambda j: near[rows, lanes(j)].astype(f32),
            lambda j: near[rows, lanes(j, FLAT)].astype(f32),
        )
        for j in range(32):
            tile = near[rows, lanes(j, 2 * FLAT)].astype(f32)
            stage_two[pl.ds(32 * j, 16), :] = tile
            stage_two[pl.ds(32 * j + 16, 16), :] = swap(tile)
        for i in range(0, 16, 2):
            at = pl.multiple_of(g * 1024 + i * 64, 128)
            after = pl.multiple_of(at + 128, 128)
            found = []
            for k, ref in enumerate((xs_ref, xe_ref)):
                weight = jnp.concatenate(
                    [matrix(stage, 16, i + k), matrix(stage_two, 16, i + k)], axis=1
                ).astype(bf16)
                vec = jnp.concatenate(
                    [ref[:, pl.ds(at, 128)], ref[:, pl.ds(after, 128)] * low16], axis=1
                )
                found.append(mmt(vec, weight))
            near_ref[:, pl.ds(at, 128)] = jnp.concatenate(found, axis=1)
        return 0

    lax.fori_loop(0, 8, near_group, 0)

    copies[1].wait()
    wide = low_lanes(64)
    even = (lax.broadcasted_iota(jnp.int32, (16, 128), 0) % 2) == 0

    def basis_group(g, _):
        rows = pl.ds(pl.multiple_of(16 * g, 16), 16)
        for j in range(32):
            tile = basis[rows, lanes(j)].astype(f32)
            turned = swap(tile)
            stage[pl.ds(32 * j, 16), :] = jnp.where(even, tile, turned)
            stage[pl.ds(32 * j + 16, 16), :] = jnp.where(even, turned, tile)
        for i in range(0, 16, 2):
            at = pl.multiple_of(g * 512 + i * 32, 64)
            basis_ref[pl.ds(at, 64), :] = jnp.where(
                wide, matrix(stage, 16, i), matrix(stage, 16, i + 1)
            ).astype(bf16)
        return 0

    lax.fori_loop(0, 8, basis_group, 0)

    copies[2].wait()
    relayout_edges(edges, stage, stage_two, highs, lows)
    vec_a[0] = highs[126].astype(f32) + lows[126].astype(f32)
    here, there = vec_a, vec_b
    nodes = 4
    while nodes <= LEAF_DEV:
        base = LEVEL_BASE[nodes]

        def children(q, here=here, there=there, base=base, final=nodes == LEAF_DEV):
            ph, plow = split(here[q])
            rh = jnp.concatenate([ph * low64, ph * high64], axis=0)
            rl = jnp.concatenate([plow * low64, plow * high64], axis=0)
            wh = highs[pl.ds(base + 2 * q, 2)].reshape(128, 128)
            wl = lows[pl.ds(base + 2 * q, 2)].reshape(128, 128)
            found = mm(wh, rh) + mm(wl, rh) + mm(wh, rl)
            if not final:
                there[2 * q] = found[:64]
                there[2 * q + 1] = found[64:]
            else:
                at = pl.multiple_of(q * 128, 128)
                down_ref[pl.ds(at, 128), :] = found.astype(bf16)

        quarter = nodes // 4
        if quarter > 4:

            def block(i, _, children=children):
                for k in range(4):
                    children(4 * i + k)
                return 0

            lax.fori_loop(0, quarter // 4, block, 0)
        else:
            for q in range(quarter):
                children(q)
        here, there = there, here
        nodes *= 2

    low = low_lanes(64)
    low32 = low_lanes(32)
    for level in range(LEVELS):
        second = couple_ref[32 * level : 32 * level + 32, :]
        first = top_ref[32 * level : 32 * level + 32, :] if level < LEVELS - 1 else second
        stage[pl.ds(64 * level, 32, stride=2), :] = jnp.where(low32, first, swap(second))
        stage[pl.ds(64 * level + 1, 32, stride=2), :] = jnp.where(low32, swap(first), second)
    chain = None
    for level in range(LEVELS):
        value = stage[64 * level : 64 * level + 64, :]
        if chain is None:
            found = value
        else:
            wh, wl = split(value)
            vh, vl = split(chain[:, :HALF])
            found = mm(vh, wh) + mm(vl, wh) + mm(vh, wl)
        chain = found
        high = found.astype(bf16).astype(f32)
        top_out_ref[level] = jnp.where(low, swap(high), found - high).astype(bf16)


def down_kernel(
    got_hbm, near_hbm, down_hbm, basis_hbm, top_ref,
    out_ref,
    got, near, down, basis, values, target, far, hats, sems,
):
    copies = [
        pltpu.make_async_copy(got_hbm, got, sems.at[0]),
        pltpu.make_async_copy(down_hbm, down, sems.at[1]),
        pltpu.make_async_copy(basis_hbm, basis, sems.at[2]),
        pltpu.make_async_copy(near_hbm, near, sems.at[3]),
    ]
    for copy in copies:
        copy.start()
    low8 = low_lanes(8)
    low16, high16 = half_masks(16)
    copies[0].wait()

    def unpack(o, _):
        for s in range(SLOTS):
            at = pl.multiple_of((o * SLOTS + s) * 8, 8)
            values[pl.ds(at, 8), :] = got[o * TILES + s].astype(f32)
        at = pl.multiple_of(o * SLOTS, 8)
        target[pl.ds(at, 8), :] = got[o * TILES + SLOTS + 1].astype(f32)
        return 0

    lax.fori_loop(0, PEERS, unpack, 0, unroll=4)
    landing = jnp.concatenate(
        [target[128 * i : 128 * i + 128, :].T for i in range(SLOTS)], axis=1
    ).astype(bf16)
    for u in range(0, 8, 2):
        chosen = jnp.concatenate(
            [values[pl.ds(u + k, PEERS * SLOTS, stride=8), :] for k in range(2)], axis=1
        ).astype(bf16)
        found = mm(landing, chosen)
        far[128 * u : 128 * u + 128, :] = found[:, :128]
        far[128 * u + 128 : 128 * u + 256, :] = found[:, 128:]

    def doubled(tile):
        turned = swap(tile)
        return jnp.concatenate(
            [jnp.where(low8, tile, turned), jnp.where(low8, turned, tile)], axis=0
        )

    me = lax.axis_index("leaf").astype(jnp.int32)
    total = jnp.zeros((2 * NV, HALF), f32)
    for level in range(LEVELS):
        parts = []
        for x in range(2**level, 2 ** (level + 1)):
            tile = got[lax.bitwise_xor(me, x) * TILES + SLOTS].astype(f32)
            if len(parts) < 4:
                parts.append(tile)
            else:
                parts[x % 4] = parts[x % 4] + tile
        tile = parts[0]
        for part in parts[1:]:
            tile = tile + part
        high, rest = split(doubled(tile))
        total = total + mmt(jnp.concatenate([high, rest * low16], axis=0), top_ref[level])
    root = total[:NV] + total[NV:]
    high, rest = split(jnp.concatenate([root, root], axis=1))
    root = jnp.concatenate([high * low16, high * high16, rest * low16, rest * high16], axis=0)

    copies[1].wait()

    def hat_block(c, _):
        at = pl.multiple_of(c * 512, 512)
        found = mmt(root, down[pl.ds(at, 512), :])
        for half in range(2):
            block = found[16 * half : 16 * half + 16] + found[32 + 16 * half : 48 + 16 * half]
            for k in range(4):
                leaf = 64 * half + 8 * c + 2 * k
                f0 = far[pl.ds(leaf, 8, stride=128), :]
                f1 = far[pl.ds(leaf + 1, 8, stride=128), :]
                gathered = jnp.concatenate(
                    [jnp.where(low8, f0, swap(f1)), jnp.where(low8, swap(f0), f1)], axis=0
                )
                to = pl.multiple_of(half * FLAT + c * 512 + k * 128, 128)
                hats[:, pl.ds(to, 128)] = (block[:, 128 * k : 128 * k + 128] + gathered).astype(
                    bf16
                )
        return 0

    lax.fori_loop(0, 8, hat_block, 0)
    copies[2].wait()
    copies[3].wait()

    def leaf_block(i, _):
        for k in range(8):
            at = pl.multiple_of(i * 1024 + k * 128, 128)
            hat = hats[:, pl.ds(at, 128)]
            weight = basis[pl.ds(pl.multiple_of(i * 512 + k * 64, 64), 64), :]
            found = mmt(jnp.concatenate([hat * low16, hat * high16], axis=0), weight)
            out_ref[:, pl.ds(at, 128)] = (
                jnp.concatenate([found[:NV], found[NV:]], axis=1) + near[:, pl.ds(at, 128)]
            )
        return 0

    lax.fori_loop(0, 8, leaf_block, 0)


def vmem():
    return pl.BlockSpec(memory_space=pltpu.VMEM)


def hbm():
    return pl.BlockSpec(memory_space=pltpu.HBM)


def params(mib):
    return pltpu.CompilerParams(vmem_limit_bytes=mib * MIB)


def shape(dims, dtype):
    return jax.ShapeDtypeStruct(dims, dtype)


def run_up(src, own, dst, x_vecs, basis, edges, top_edges, pairs):
    return pl.pallas_call(
        up_kernel,
        name="up",
        out_shape=(shape((PEERS * TILES, 8, 128), bf16), shape((8, 128), f32)),
        in_specs=[vmem(), vmem(), hbm(), hbm(), hbm(), hbm(), hbm(), hbm()],
        out_specs=(vmem(), vmem()),
        scratch_shapes=[
            pltpu.SMEM((PAIR_ROWS,), jnp.int32),
            pltpu.SMEM((PAIR_ROWS,), jnp.int32),
            pltpu.SMEM((PAIR_ROWS,), jnp.int32),
            pltpu.VMEM((LEAF_DEV, FLAT), bf16),
            pltpu.VMEM((EDGE_ROWS, FLAT), f32),
            pltpu.VMEM((PAIR_ROWS, FLAT), bf16),
            pltpu.VMEM((1024, 128), f32),
            pltpu.VMEM((1024, 128), f32),
            pltpu.VMEM((64 * (LEVELS - 1), 128), f32),
            pltpu.VMEM((64, NV, 128), f32),
            pltpu.VMEM((64, NV, 128), f32),
            pltpu.VMEM((128, 64, 128), bf16),
            pltpu.VMEM((128, 64, 128), bf16),
            pltpu.VMEM((LEAF_DEV, NV, 128), bf16),
            pltpu.VMEM((PEERS * SLOTS, 128), f32),
            pltpu.SMEM((PEERS,), jnp.int32),
            pltpu.SemaphoreType.DMA((6,)),
        ],
        compiler_params=params(60),
        cost_estimate=pl.CostEstimate(
            flops=10**9, bytes_accessed=12 * 10**6, transcendentals=0
        ),
    )(x_vecs, top_edges, src, own, dst, basis, edges, pairs)


def run_mid(after, xs, xe, near, basis, edges, top, couple):
    return pl.pallas_call(
        mid_kernel,
        name="mid",
        out_shape=(
            shape((NV, LEAF_DEV * LEAF), f32),
            shape((LEAF_DEV * RANK // 2, 128), bf16),
            shape((LEAF_DEV * LEAF // 2, 128), bf16),
            shape((LEVELS, RANK, 128), bf16),
        ),
        in_specs=[vmem(), vmem(), vmem(), hbm(), hbm(), hbm(), vmem(), vmem()],
        out_specs=(vmem(), vmem(), vmem(), vmem()),
        scratch_shapes=[
            pltpu.VMEM((LEAF_DEV, 3 * FLAT), bf16),
            pltpu.VMEM((LEAF_DEV, FLAT), bf16),
            pltpu.VMEM((EDGE_ROWS, FLAT), f32),
            pltpu.VMEM((1024, 128), f32),
            pltpu.VMEM((1024, 128), f32),
            pltpu.VMEM((64, 64, 128), f32),
            pltpu.VMEM((64, 64, 128), f32),
            pltpu.VMEM((128, 64, 128), bf16),
            pltpu.VMEM((128, 64, 128), bf16),
            pltpu.SemaphoreType.DMA((3,)),
        ],
        compiler_params=params(60),
        cost_estimate=pl.CostEstimate(
            flops=10**9, bytes_accessed=14 * 10**6, transcendentals=0
        ),
    )(after, xs, xe, near, basis, edges, top, couple)


def run_down(got, near, down, basis, top):
    return pl.pallas_call(
        down_kernel,
        name="down",
        out_shape=shape((NV, LEAF_DEV * LEAF), f32),
        in_specs=[
            pl.BlockSpec(memory_space=pl.ANY),
            hbm(),
            hbm(),
            hbm(),
            vmem(),
        ],
        out_specs=vmem(),
        scratch_shapes=[
            pltpu.VMEM((PEERS * TILES, 8, 128), bf16),
            pltpu.VMEM((NV, LEAF_DEV * LEAF), f32),
            pltpu.VMEM((LEAF_DEV * RANK // 2, 128), bf16),
            pltpu.VMEM((LEAF_DEV * LEAF // 2, 128), bf16),
            pltpu.VMEM((PEERS * SLOTS * 8, 128), f32),
            pltpu.VMEM((PEERS * SLOTS, 128), f32),
            pltpu.VMEM((8 * LEAF_DEV, 128), f32),
            pltpu.VMEM((NV, LEAF_DEV * LEAF), bf16),
            pltpu.SemaphoreType.DMA((4,)),
        ],
        compiler_params=params(59),
        cost_estimate=pl.CostEstimate(
            flops=10**9, bytes_accessed=8 * 10**6, transcendentals=0
        ),
    )(got, near, down, basis, top)


def shards(
    x_vecs,
    leaf_basis,
    near_blocks,
    local_edges,
    top_edges,
    top_couple,
    couple_blocks,
    couple_src,
    couple_owner,
    couple_dst,
):
    ahead = [(i, (i + 1) % PEERS) for i in range(PEERS)]
    back = [(target, source) for source, target in ahead]
    before = lax.ppermute(x_vecs[:, -LEAF:], "leaf", ahead)
    following = lax.ppermute(x_vecs[:, :LEAF], "leaf", back)
    top_flat = top_edges.reshape((LEVELS - 1) * 32, 128)
    outgoing, after = run_up(
        couple_src, couple_owner.reshape(PAIR_ROWS), couple_dst, x_vecs, leaf_basis,
        local_edges, top_flat, couple_blocks,
    )
    outgoing, before, following = lax.optimization_barrier((outgoing, before, following))
    got = lax.all_to_all(
        outgoing.reshape(PEERS, TILES * 8, 128), "leaf", split_axis=0, concat_axis=0, tiled=True
    ).reshape(PEERS * TILES, 8, 128)
    fill = jnp.zeros((NV, LEAF), bf16)
    xs = jnp.concatenate([before, x_vecs, following], axis=1)
    xe = jnp.concatenate([x_vecs, following, fill], axis=1)
    near, down, basis, tops = run_mid(
        after, xs, xe, near_blocks, leaf_basis, local_edges, top_flat,
        top_couple.reshape(LEVELS * 32, 128),
    )
    return run_down(got, near, down, basis, tops)


def solution(mesh):
    return jax.shard_map(
        shards,
        mesh=mesh,
        in_specs=(
            P(None, "leaf"),
            P("leaf", None),
            P("leaf", None),
            P("leaf", None),
            P("leaf", None, None),
            P("leaf", None, None),
            P("leaf", None),
            P("leaf"),
            P("leaf", None),
            P("leaf"),
        ),
        out_specs=P(None, "leaf"),
        check_vma=False,
    )
```

```python
import jax
import jax.numpy as jnp
from jax import lax
from jax.experimental import pallas as pl
from jax.experimental.pallas import tpu as pltpu
from jax.sharding import PartitionSpec as P

LEAF = 64
RANK = 64
NV = 16
LEAF_DEV = 128
PEERS = 128
LEVELS = 7
SLOTS = 8
TILES = SLOTS + 2
PAIR_ROWS = 512
CHUNKS = 4
EDGE_ROWS = 254
FLAT = 4096
HALF = 64
MIB = 1024 * 1024

LEVEL_BASE = {128: 0, 64: 64, 32: 96, 16: 112, 8: 120, 4: 124, 2: 126}

f32 = jnp.float32
bf16 = jnp.bfloat16


def low_lanes(rows):
    return lax.broadcasted_iota(jnp.int32, (rows, 128), 1) < HALF


def half_masks(rows):
    low = low_lanes(rows).astype(f32)
    return low.astype(bf16), (1.0 - low).astype(bf16)


def swap(value):
    return pltpu.roll(value, HALF, 1)


def join(first, second):
    return jnp.where(low_lanes(first.shape[0]), first, swap(second))


def split(value):
    high = value.astype(bf16)
    return high, (value - high.astype(f32)).astype(bf16)


def mm(left, right):
    return jnp.dot(left, right, preferred_element_type=f32)


def mmt(left, right):
    return lax.dot_general(left, right, (((1,), (1,)), ((), ())), preferred_element_type=f32)


def paired(stage, group, load_first, load_second):
    low = low_lanes(group)
    for j in range(32):
        first = load_first(j)
        second = load_second(j)
        stage[pl.ds(2 * j * group, group), :] = jnp.where(low, first, swap(second))
        stage[pl.ds((2 * j + 1) * group, group), :] = jnp.where(low, swap(first), second)


def matrix(stage, group, index):
    return stage[pl.ds(index, 64, stride=group), :]


def lanes(j, start=0):
    return pl.ds(start + j * 128, 128)


def relayout_edges(edges, stage, stage_two, highs, lows):
    def keep(at, index, place):
        high, low = split(matrix(at, 8, index))
        highs[place] = high
        lows[place] = low

    def layout(g, to):
        first = jnp.where(
            g < 8, 8 * g, jnp.where(g < 12, 64 + 8 * g, jnp.where(g < 14, 96 + 8 * g, 224))
        )
        gap = jnp.where(g < 8, 64, jnp.where(g < 12, 32, jnp.where(g < 14, 16, 8)))
        first = pl.multiple_of(first, 8)
        second = pl.multiple_of(first + gap, 8)
        paired(
            to,
            8,
            lambda j: edges[pl.ds(first, 8), lanes(j)],
            lambda j: edges[pl.ds(second, 8), lanes(j)],
        )

    def step(h, _):
        odd = jnp.minimum(2 * h + 1, 14)
        layout(2 * h, stage)
        layout(odd, stage_two)
        for i in range(8):
            keep(stage, i, 16 * h + i)
        for i in range(8):
            keep(stage_two, i, 8 * odd + i)
        return 0

    lax.fori_loop(0, 8, step, 0)
    paired(
        stage,
        8,
        lambda j: edges[240:248, lanes(j)],
        lambda j: pltpu.roll(edges[240:248, lanes(j)], 4, 0),
    )
    rows = lax.broadcasted_iota(jnp.int32, (8, 128), 0)

    def last_second(j):
        tile = edges[246:254, lanes(j)]
        return jnp.where(rows < 6, pltpu.roll(tile, 6, 0), pltpu.roll(tile, 7, 0))

    paired(stage_two, 8, lambda j: edges[246:254, lanes(j)], last_second)
    for i in range(4):
        keep(stage, i, 120 + i)
    keep(stage_two, 2, 124)
    keep(stage_two, 3, 125)
    keep(stage_two, 6, 126)


def up_kernel(
    x_ref, top_ref, src_hbm, own_hbm, dst_hbm, basis_hbm, edges_hbm, pairs_hbm,
    out_ref, done_ref,
    src_ref, own_ref, dst_ref, basis, edges, pairs, stage, stage_two, tops, vec_a, vec_b,
    highs, lows, table, rows_at, count, sems,
):
    basis_copy = pltpu.make_async_copy(basis_hbm, basis, sems.at[0])
    edges_copy = pltpu.make_async_copy(edges_hbm, edges, sems.at[1])
    pairs_copy = pltpu.make_async_copy(pairs_hbm, pairs, sems.at[2])
    lists = [
        pltpu.make_async_copy(src_hbm, src_ref, sems.at[3]),
        pltpu.make_async_copy(own_hbm, own_ref, sems.at[4]),
        pltpu.make_async_copy(dst_hbm, dst_ref, sems.at[5]),
    ]
    basis_copy.start()
    edges_copy.start()
    for copy in lists:
        copy.start()
    low16, high16 = half_masks(16)
    low = low_lanes(16)

    def clear(i, _):
        out_ref[pl.ds(i * 32, 32)] = jnp.zeros((32, 8, 128), bf16)
        return 0

    lax.fori_loop(0, PEERS * TILES // 32, clear, 0)
    rows_at[...] = jnp.zeros_like(rows_at)

    def clear_count(i, _):
        for k in range(16):
            count[16 * i + k] = 0
        return 0

    lax.fori_loop(0, PEERS // 16, clear_count, 0)
    for level in range(LEVELS - 1):
        tile = top_ref[32 * level : 32 * level + 32, :]
        tops[pl.ds(64 * level, 32, stride=2), :] = tile
        tops[pl.ds(64 * level + 1, 32, stride=2), :] = swap(tile)

    basis_copy.wait()
    pairs_copy.start()

    def leaf_layout(g, to):
        first = pl.multiple_of(16 * g, 16)
        second = pl.multiple_of(64 + 16 * g, 16)
        paired(
            to,
            16,
            lambda j: basis[pl.ds(first, 16), lanes(j)].astype(f32),
            lambda j: basis[pl.ds(second, 16), lanes(j)].astype(f32),
        )

    def leaf_products(g, at_stage):
        for i in range(0, 16, 2):
            weight = jnp.concatenate([matrix(at_stage, 16, i), matrix(at_stage, 16, i + 1)], axis=0)
            at = pl.multiple_of(g * 1024 + i * 64, 128)
            left = x_ref[:, pl.ds(at, 128)]
            right = x_ref[:, pl.ds(pl.multiple_of(at + FLAT, 128), 128)]
            stacked = jnp.concatenate(
                [left * low16, right * low16, left * high16, right * high16], axis=0
            )
            found = mm(stacked, weight.astype(bf16))
            for k in range(2):
                pair = jnp.where(low, found[32 * k : 32 * k + 16], found[32 * k + 16 : 32 * k + 32])
                turned = swap(pair)
                t = 16 * g + i + k
                vec_a[t] = pair
                table[t] = jnp.where(low, pair, turned).astype(bf16)
                table[t + 64] = jnp.where(low, turned, pair).astype(bf16)

    def leaf_step(h, _):
        leaf_layout(2 * h, stage)
        leaf_layout(2 * h + 1, stage_two)
        leaf_products(2 * h, stage)
        leaf_products(2 * h + 1, stage_two)
        return 0

    lax.fori_loop(0, 2, leaf_step, 0)

    edges_copy.wait()
    relayout_edges(edges, stage, stage_two, highs, lows)

    def parents(nodes, first, amount):
        up = nodes in (128, 32, 8)
        here, there = (vec_a, vec_b) if up else (vec_b, vec_a)
        base = LEVEL_BASE[nodes]
        for k in range(amount):
            q = first + k
            p0 = here[2 * q]
            p1 = here[2 * q + 1]
            both = jnp.concatenate(
                [jnp.where(low, p0, swap(p1)), jnp.where(low, swap(p0), p1)], axis=0
            )
            vh, vl = split(both)
            wh = highs[pl.ds(base + 2 * q, 2)].reshape(128, 128)
            wl = lows[pl.ds(base + 2 * q, 2)].reshape(128, 128)
            two = mm(jnp.concatenate([vh, vl], axis=0), wh)
            found = two[:32] + two[32:] + mm(vh, wl)
            there[q] = jnp.where(low, found[:16], found[16:])

    def root():
        last = vec_a[0]
        both = jnp.concatenate([last, swap(last)], axis=0)[:, :HALF]
        vh, vl = split(both)
        two = mm(jnp.concatenate([vh, vl], axis=0), highs[126])
        found = two[:32] + two[32:] + mm(vh, lows[126])
        return found[:16] + swap(found[16:])

    def carried(current, level):
        wh, wl = split(tops[64 * level : 64 * level + 64, :])
        vh, vl = split(current[:, :HALF])
        two = mm(jnp.concatenate([vh, vl], axis=0), wh)
        return two[:16] + two[16:] + mm(vh, wl)

    me = lax.axis_index("leaf").astype(jnp.int32)

    def send(current, level):
        tile = join(current[0:8], current[8:16]).astype(bf16)
        for x in range(2**level, 2 ** (level + 1)):
            out_ref[lax.bitwise_xor(me, x) * TILES + SLOTS] = tile

    for copy in lists:
        copy.wait()
    pairs_copy.wait()
    lane_ids = lax.broadcasted_iota(jnp.int32, (1, 128), 1)

    def pair_layout(g, to):
        first = pl.multiple_of(32 * g, 16)
        second = pl.multiple_of(32 * g + 16, 16)
        paired(
            to,
            16,
            lambda j: pairs[pl.ds(first, 16), lanes(j)].astype(f32),
            lambda j: pairs[pl.ds(second, 16), lanes(j)].astype(f32),
        )

    def pair_products(g, at):
        zero = jnp.zeros((32, 128), bf16)
        for i in range(0, 16, 2):
            weight = jnp.concatenate(
                [matrix(at, 16, i), matrix(at, 16, i + 1)], axis=1
            ).astype(bf16)
            listed = [32 * g + i, 32 * g + 16 + i, 32 * g + i + 1, 32 * g + 17 + i]
            sources = [table[src_ref[r]] for r in listed]
            first = jnp.concatenate([sources[0] * low16, sources[1] * high16], axis=0)
            second = jnp.concatenate([sources[2] * low16, sources[3] * high16], axis=0)
            stacked = jnp.concatenate(
                [
                    jnp.concatenate([first, zero], axis=1),
                    jnp.concatenate([zero, second], axis=1),
                ],
                axis=0,
            )
            found = mmt(stacked, weight)
            for k in range(4):
                owner = own_ref[listed[k]]
                rank = count[owner]
                count[owner] = rank + 1
                tile = jnp.concatenate(
                    [found[16 * k : 16 * k + 8], found[16 * k + 8 : 16 * k + 16]], axis=1
                )
                out_ref[owner * TILES + rank] = tile.astype(bf16)
                rows_at[pl.ds(owner * SLOTS + rank, 1), :] = jnp.where(
                    lane_ids == dst_ref[listed[k]], 1.0, 0.0
                )

    groups = PAIR_ROWS // 32
    pair_layout(0, stage)

    def pair_step(h):
        pair_layout(2 * h + 1, stage_two)
        pair_products(2 * h, stage)
        pair_layout(jnp.minimum(2 * h + 2, groups - 1), stage)
        pair_products(2 * h + 1, stage_two)

    def first_steps(h, _):
        parents(128, 8 * h, 8)
        pair_step(h)
        return 0

    lax.fori_loop(0, 4, first_steps, 0)
    parents(64, 0, 16)
    pair_step(4)
    parents(32, 0, 8)
    parents(16, 0, 4)
    pair_step(5)
    parents(8, 0, 2)
    parents(4, 0, 1)
    current = root()
    send(current, 0)
    current = carried(current, 0)
    pair_step(6)
    for level in range(1, LEVELS):
        send(current, level)
        if level < LEVELS - 1:
            current = carried(current, level)
    pair_step(7)

    def place_rows(o, _):
        out_ref[o * TILES + SLOTS + 1] = rows_at[
            pl.ds(pl.multiple_of(o * SLOTS, 8), 8), :
        ].astype(bf16)
        return 0

    lax.fori_loop(0, PEERS, place_rows, 0, unroll=16)
    done_ref[...] = current[0:8]


def mid_kernel(
    after_ref, xs_ref, xe_ref, near_hbm, basis_hbm, edges_hbm, top_ref, couple_ref,
    near_ref, down_ref, basis_ref, top_out_ref, ends_ref,
    near, basis, edges, stage, stage_two, vec_a, vec_b, highs, lows, sems,
):
    copies = [
        pltpu.make_async_copy(near_hbm, near, sems.at[0]),
        pltpu.make_async_copy(basis_hbm, basis, sems.at[1]),
        pltpu.make_async_copy(edges_hbm, edges, sems.at[2]),
    ]
    for copy in copies:
        copy.start()
    low16, _ = half_masks(16)
    low64, high64 = half_masks(64)

    copies[0].wait()

    def near_group(g, _):
        first = pl.multiple_of(16 * g, 16)
        rows = pl.ds(first, 16)
        paired(
            stage,
            16,
            lambda j: near[rows, lanes(j)].astype(f32),
            lambda j: near[rows, lanes(j, FLAT)].astype(f32),
        )
        for j in range(32):
            tile = near[rows, lanes(j, 2 * FLAT)].astype(f32)
            stage_two[pl.ds(32 * j, 16), :] = tile
            stage_two[pl.ds(32 * j + 16, 16), :] = swap(tile)
        for i in range(0, 16, 2):
            at = pl.multiple_of(g * 1024 + i * 64, 128)
            after = pl.multiple_of(at + 128, 128)
            found = []
            for k, ref in enumerate((xs_ref, xe_ref)):
                weight = jnp.concatenate(
                    [matrix(stage, 16, i + k), matrix(stage_two, 16, i + k)], axis=1
                ).astype(bf16)
                vec = jnp.concatenate(
                    [ref[:, pl.ds(at, 128)], ref[:, pl.ds(after, 128)] * low16], axis=1
                )
                found.append(mmt(vec, weight))
            near_ref[:, pl.ds(at, 128)] = jnp.concatenate(found, axis=1)

        @pl.when(g == 0)
        def _():
            vec_a[0] = matrix(stage, 16, 0)

        return 0

    lax.fori_loop(0, 8, near_group, 0)
    ends_ref[...] = join(vec_a[0], matrix(stage_two, 16, 15)).astype(bf16)

    copies[1].wait()
    wide = low_lanes(64)
    even = (lax.broadcasted_iota(jnp.int32, (16, 128), 0) % 2) == 0

    def basis_group(g, _):
        rows = pl.ds(pl.multiple_of(16 * g, 16), 16)
        for j in range(32):
            tile = basis[rows, lanes(j)].astype(f32)
            turned = swap(tile)
            stage[pl.ds(32 * j, 16), :] = jnp.where(even, tile, turned)
            stage[pl.ds(32 * j + 16, 16), :] = jnp.where(even, turned, tile)
        for i in range(0, 16, 2):
            at = pl.multiple_of(g * 512 + i * 32, 64)
            basis_ref[pl.ds(at, 64), :] = jnp.where(
                wide, matrix(stage, 16, i), matrix(stage, 16, i + 1)
            ).astype(bf16)
        return 0

    lax.fori_loop(0, 8, basis_group, 0)

    copies[2].wait()
    relayout_edges(edges, stage, stage_two, highs, lows)
    vec_a[0] = highs[126].astype(f32) + lows[126].astype(f32)
    here, there = vec_a, vec_b
    nodes = 4
    while nodes <= LEAF_DEV:
        base = LEVEL_BASE[nodes]

        def children(q, here=here, there=there, base=base, final=nodes == LEAF_DEV):
            ph, plow = split(here[q])
            rh = jnp.concatenate([ph * low64, ph * high64], axis=0)
            rl = jnp.concatenate([plow * low64, plow * high64], axis=0)
            wh = highs[pl.ds(base + 2 * q, 2)].reshape(128, 128)
            wl = lows[pl.ds(base + 2 * q, 2)].reshape(128, 128)
            found = mm(wh, rh) + mm(wl, rh) + mm(wh, rl)
            if not final:
                there[2 * q] = found[:64]
                there[2 * q + 1] = found[64:]
            else:
                at = pl.multiple_of(q * 128, 128)
                down_ref[pl.ds(at, 128), :] = found.astype(bf16)

        quarter = nodes // 4
        if quarter > 4:

            def block(i, _, children=children):
                for k in range(4):
                    children(4 * i + k)
                return 0

            lax.fori_loop(0, quarter // 4, block, 0)
        else:
            for q in range(quarter):
                children(q)
        here, there = there, here
        nodes *= 2

    low = low_lanes(64)
    low32 = low_lanes(32)
    for level in range(LEVELS):
        second = couple_ref[32 * level : 32 * level + 32, :]
        first = top_ref[32 * level : 32 * level + 32, :] if level < LEVELS - 1 else second
        stage[pl.ds(64 * level, 32, stride=2), :] = jnp.where(low32, first, swap(second))
        stage[pl.ds(64 * level + 1, 32, stride=2), :] = jnp.where(low32, swap(first), second)
    chain = None
    for level in range(LEVELS):
        value = stage[64 * level : 64 * level + 64, :]
        if chain is None:
            found = value
        else:
            wh, wl = split(value)
            vh, vl = split(chain[:, :HALF])
            found = mm(vh, wh) + mm(vl, wh) + mm(vh, wl)
        chain = found
        high = found.astype(bf16).astype(f32)
        top_out_ref[level] = jnp.where(low, swap(high), found - high).astype(bf16)


def down_kernel(
    got_hbm, near_hbm, down_hbm, basis_hbm, top_ref, ends_ref, before_ref, following_ref,
    out_ref,
    got, near, down, basis, values, target, far, sems,
):
    span = PEERS // CHUNKS
    arriving = [
        pltpu.make_async_copy(
            got_hbm.at[pl.ds(c * span * TILES, span * TILES)],
            got.at[pl.ds(c * span * TILES, span * TILES)],
            sems.at[c],
        )
        for c in range(CHUNKS)
    ]
    copies = [
        pltpu.make_async_copy(down_hbm, down, sems.at[CHUNKS]),
        pltpu.make_async_copy(basis_hbm, basis, sems.at[CHUNKS + 1]),
        pltpu.make_async_copy(near_hbm, near, sems.at[CHUNKS + 2]),
    ]
    for copy in arriving:
        copy.start()
    low8 = low_lanes(8)
    low16, high16 = half_masks(16)

    def unpack(o, _):
        for s in range(SLOTS):
            at = pl.multiple_of((o * SLOTS + s) * 8, 8)
            values[pl.ds(at, 8), :] = got[o * TILES + s].astype(f32)
        at = pl.multiple_of(o * SLOTS, 8)
        target[pl.ds(at, 8), :] = got[o * TILES + SLOTS + 1].astype(f32)
        return 0

    for c in range(CHUNKS):
        arriving[c].wait()
        if c == CHUNKS - 2:
            for copy in copies:
                copy.start()
        lax.fori_loop(c * span, (c + 1) * span, unpack, 0, unroll=4)
    landing = jnp.concatenate(
        [target[128 * i : 128 * i + 128, :].T for i in range(SLOTS)], axis=1
    ).astype(bf16)
    for u in range(0, 8, 2):
        chosen = jnp.concatenate(
            [values[pl.ds(u + k, PEERS * SLOTS, stride=8), :] for k in range(2)], axis=1
        ).astype(bf16)
        found = mm(landing, chosen)
        far[128 * u : 128 * u + 128, :] = found[:, :128]
        far[128 * u + 128 : 128 * u + 256, :] = found[:, 128:]

    def doubled(tile):
        turned = swap(tile)
        return jnp.concatenate(
            [jnp.where(low8, tile, turned), jnp.where(low8, turned, tile)], axis=0
        )

    me = lax.axis_index("leaf").astype(jnp.int32)
    total = jnp.zeros((2 * NV, HALF), f32)
    for level in range(LEVELS):
        parts = []
        for x in range(2**level, 2 ** (level + 1)):
            tile = got[lax.bitwise_xor(me, x) * TILES + SLOTS].astype(f32)
            if len(parts) < 4:
                parts.append(tile)
            else:
                parts[x % 4] = parts[x % 4] + tile
        tile = parts[0]
        for part in parts[1:]:
            tile = tile + part
        high, rest = split(doubled(tile))
        total = total + mmt(jnp.concatenate([high, rest * low16], axis=0), top_ref[level])
    root = total[:NV] + total[NV:]
    high, rest = split(jnp.concatenate([root, root], axis=1))
    root = jnp.concatenate([high * low16, high * high16, rest * low16, rest * high16], axis=0)

    for copy in copies:
        copy.wait()
    zero = jnp.zeros((2 * NV, 128), bf16)
    for c in range(8):
        found = mmt(root, down[512 * c : 512 * c + 512, :])
        for half in range(2):
            block = found[16 * half : 16 * half + 16] + found[32 + 16 * half : 48 + 16 * half]
            pieces = []
            for k in range(4):
                leaf = 64 * half + 8 * c + 2 * k
                f0 = far[pl.ds(leaf, 8, stride=128), :]
                f1 = far[pl.ds(leaf + 1, 8, stride=128), :]
                gathered = jnp.concatenate(
                    [jnp.where(low8, f0, swap(f1)), jnp.where(low8, swap(f0), f1)], axis=0
                )
                hat = (block[:, 128 * k : 128 * k + 128] + gathered).astype(bf16)
                pieces.append(jnp.concatenate([hat * low16, hat * high16], axis=0))
            for k in range(0, 4, 2):
                leaf = 64 * half + 8 * c + 2 * k
                stacked = jnp.concatenate(
                    [
                        jnp.concatenate([pieces[k], zero], axis=1),
                        jnp.concatenate([zero, pieces[k + 1]], axis=1),
                    ],
                    axis=0,
                )
                weight = jnp.concatenate(
                    [
                        basis[32 * leaf : 32 * leaf + 64, :],
                        basis[32 * leaf + 64 : 32 * leaf + 128, :],
                    ],
                    axis=1,
                )
                part = mmt(stacked, weight)
                for m in range(2):
                    at = 64 * leaf + 128 * m
                    out_ref[:, at : at + 128] = (
                        jnp.concatenate(
                            [part[32 * m : 32 * m + 16], part[32 * m + 16 : 32 * m + 32]], axis=1
                        )
                        + near[:, at : at + 128]
                    )
    edge = jnp.zeros((NV, HALF), f32)
    out_ref[:, :128] += jnp.concatenate([mmt(before_ref[...], ends_ref[:, :HALF]), edge], axis=1)
    out_ref[:, 8064:] += jnp.concatenate(
        [edge, mmt(following_ref[...], ends_ref[:, HALF:])], axis=1
    )


def vmem():
    return pl.BlockSpec(memory_space=pltpu.VMEM)


def hbm():
    return pl.BlockSpec(memory_space=pltpu.HBM)


def params(mib):
    return pltpu.CompilerParams(vmem_limit_bytes=mib * MIB)


def shape(dims, dtype):
    return jax.ShapeDtypeStruct(dims, dtype)


def run_up(src, own, dst, x_vecs, basis, edges, top_edges, pairs):
    return pl.pallas_call(
        up_kernel,
        name="up",
        out_shape=(shape((PEERS * TILES, 8, 128), bf16), shape((8, 128), f32)),
        in_specs=[vmem(), vmem(), hbm(), hbm(), hbm(), hbm(), hbm(), hbm()],
        out_specs=(vmem(), vmem()),
        scratch_shapes=[
            pltpu.SMEM((PAIR_ROWS,), jnp.int32),
            pltpu.SMEM((PAIR_ROWS,), jnp.int32),
            pltpu.SMEM((PAIR_ROWS,), jnp.int32),
            pltpu.VMEM((LEAF_DEV, FLAT), bf16),
            pltpu.VMEM((EDGE_ROWS, FLAT), f32),
            pltpu.VMEM((PAIR_ROWS, FLAT), bf16),
            pltpu.VMEM((1024, 128), f32),
            pltpu.VMEM((1024, 128), f32),
            pltpu.VMEM((64 * (LEVELS - 1), 128), f32),
            pltpu.VMEM((64, NV, 128), f32),
            pltpu.VMEM((64, NV, 128), f32),
            pltpu.VMEM((128, 64, 128), bf16),
            pltpu.VMEM((128, 64, 128), bf16),
            pltpu.VMEM((LEAF_DEV, NV, 128), bf16),
            pltpu.VMEM((PEERS * SLOTS, 128), f32),
            pltpu.SMEM((PEERS,), jnp.int32),
            pltpu.SemaphoreType.DMA((6,)),
        ],
        compiler_params=params(60),
        cost_estimate=pl.CostEstimate(
            flops=10**9, bytes_accessed=12 * 10**6, transcendentals=0
        ),
    )(x_vecs, top_edges, src, own, dst, basis, edges, pairs)


def run_mid(after, xs, xe, near, basis, edges, top, couple):
    return pl.pallas_call(
        mid_kernel,
        name="mid",
        out_shape=(
            shape((NV, LEAF_DEV * LEAF), f32),
            shape((LEAF_DEV * RANK // 2, 128), bf16),
            shape((LEAF_DEV * LEAF // 2, 128), bf16),
            shape((LEVELS, RANK, 128), bf16),
            shape((LEAF, 128), bf16),
        ),
        in_specs=[vmem(), vmem(), vmem(), hbm(), hbm(), hbm(), vmem(), vmem()],
        out_specs=(vmem(), vmem(), vmem(), vmem(), vmem()),
        scratch_shapes=[
            pltpu.VMEM((LEAF_DEV, 3 * FLAT), bf16),
            pltpu.VMEM((LEAF_DEV, FLAT), bf16),
            pltpu.VMEM((EDGE_ROWS, FLAT), f32),
            pltpu.VMEM((1024, 128), f32),
            pltpu.VMEM((1024, 128), f32),
            pltpu.VMEM((64, 64, 128), f32),
            pltpu.VMEM((64, 64, 128), f32),
            pltpu.VMEM((128, 64, 128), bf16),
            pltpu.VMEM((128, 64, 128), bf16),
            pltpu.SemaphoreType.DMA((3,)),
        ],
        compiler_params=params(62),
        cost_estimate=pl.CostEstimate(
            flops=10**9, bytes_accessed=14 * 10**6, transcendentals=0
        ),
    )(after, xs, xe, near, basis, edges, top, couple)


def run_down(got, near, down, basis, top, ends, before, following):
    return pl.pallas_call(
        down_kernel,
        name="down",
        out_shape=shape((NV, LEAF_DEV * LEAF), f32),
        in_specs=[hbm(), hbm(), hbm(), hbm(), vmem(), vmem(), vmem(), vmem()],
        out_specs=vmem(),
        scratch_shapes=[
            pltpu.VMEM((PEERS * TILES, 8, 128), bf16),
            pltpu.VMEM((NV, LEAF_DEV * LEAF), f32),
            pltpu.VMEM((LEAF_DEV * RANK // 2, 128), bf16),
            pltpu.VMEM((LEAF_DEV * LEAF // 2, 128), bf16),
            pltpu.VMEM((PEERS * SLOTS * 8, 128), f32),
            pltpu.VMEM((PEERS * SLOTS, 128), f32),
            pltpu.VMEM((8 * LEAF_DEV, 128), f32),
            pltpu.SemaphoreType.DMA((CHUNKS + 3,)),
        ],
        compiler_params=params(59),
        cost_estimate=pl.CostEstimate(
            flops=10**9, bytes_accessed=8 * 10**6, transcendentals=0
        ),
    )(got, near, down, basis, top, ends, before, following)


def shards(
    x_vecs,
    leaf_basis,
    near_blocks,
    local_edges,
    top_edges,
    top_couple,
    couple_blocks,
    couple_src,
    couple_owner,
    couple_dst,
):
    top_flat = top_edges.reshape((LEVELS - 1) * 32, 128)
    outgoing, after = run_up(
        couple_src, couple_owner.reshape(PAIR_ROWS), couple_dst, x_vecs, leaf_basis,
        local_edges, top_flat, couple_blocks,
    )
    first, last, after = lax.optimization_barrier((x_vecs[:, :LEAF], x_vecs[:, -LEAF:], after))
    ahead = [(i, (i + 1) % PEERS) for i in range(PEERS)]
    back = [(target, source) for source, target in ahead]
    before = lax.ppermute(last, "leaf", ahead)
    following = lax.ppermute(first, "leaf", back)
    got = lax.all_to_all(
        outgoing.reshape(PEERS, TILES * 8, 128), "leaf", split_axis=0, concat_axis=0, tiled=True
    ).reshape(PEERS * TILES, 8, 128)
    fill = jnp.zeros((NV, LEAF), bf16)
    xs = jnp.concatenate([fill, x_vecs, fill], axis=1)
    xe = jnp.concatenate([x_vecs, fill, fill], axis=1)
    near, down, basis, tops, ends = run_mid(
        after, xs, xe, near_blocks, leaf_basis, local_edges, top_flat,
        top_couple.reshape(LEVELS * 32, 128),
    )
    return run_down(got, near, down, basis, tops, ends, before, following)


def solution(mesh):
    return jax.shard_map(
        shards,
        mesh=mesh,
        in_specs=(
            P(None, "leaf"),
            P("leaf", None),
            P("leaf", None),
            P("leaf", None),
            P("leaf", None, None),
            P("leaf", None, None),
            P("leaf", None),
            P("leaf"),
            P("leaf", None),
            P("leaf"),
        ),
        out_specs=P(None, "leaf"),
        check_vma=False,
    )
```

```python
import jax
import jax.numpy as jnp
from jax import lax
from jax.experimental import pallas as pl
from jax.experimental.pallas import tpu as pltpu
from jax.sharding import PartitionSpec as P

LEAF = 64
RANK = 64
NV = 16
LEAF_DEV = 128
PEERS = 128
LEVELS = 7
SLOTS = 8
TILES = SLOTS + 2
PAIR_ROWS = 512
CHUNKS = 4
EDGE_ROWS = 254
FLAT = 4096
HALF = 64
MIB = 1024 * 1024

LEVEL_BASE = {128: 0, 64: 64, 32: 96, 16: 112, 8: 120, 4: 124, 2: 126}

f32 = jnp.float32
bf16 = jnp.bfloat16


def low_lanes(rows):
    return lax.broadcasted_iota(jnp.int32, (rows, 128), 1) < HALF


def half_masks(rows):
    low = low_lanes(rows).astype(f32)
    return low.astype(bf16), (1.0 - low).astype(bf16)


def swap(value):
    return pltpu.roll(value, HALF, 1)


def join(first, second):
    return jnp.where(low_lanes(first.shape[0]), first, swap(second))


def split(value):
    high = value.astype(bf16)
    return high, (value - high.astype(f32)).astype(bf16)


def mm(left, right):
    return jnp.dot(left, right, preferred_element_type=f32)


def mmt(left, right):
    return lax.dot_general(left, right, (((1,), (1,)), ((), ())), preferred_element_type=f32)


def paired(stage, group, load_first, load_second):
    low = low_lanes(group)
    for j in range(32):
        first = load_first(j)
        second = load_second(j)
        stage[pl.ds(2 * j * group, group), :] = jnp.where(low, first, swap(second))
        stage[pl.ds((2 * j + 1) * group, group), :] = jnp.where(low, swap(first), second)


def paired_half(stage, load_first, load_second):
    for j in range(32):
        first = load_first(j)
        second = load_second(j)
        stage[pl.ds(32 * j, 16), :] = jnp.concatenate(
            [first[:, :HALF], second[:, :HALF]], axis=1
        ).astype(f32)
        stage[pl.ds(32 * j + 16, 16), :] = jnp.concatenate(
            [first[:, HALF:], second[:, HALF:]], axis=1
        ).astype(f32)


def matrix(stage, group, index):
    return stage[pl.ds(index, 64, stride=group), :]


def lanes(j, start=0):
    return pl.ds(start + j * 128, 128)


def edge_steps(edges, stage, stage_two, highs, lows):
    def keep(at, index, place):
        high, low = split(matrix(at, 8, index))
        highs[place] = high
        lows[place] = low

    def layout(g, to):
        if isinstance(g, int):
            first, gap = 8 * g, 64
            if g >= 8:
                first, gap = (64 + 8 * g, 32) if g < 12 else (96 + 8 * g, 16) if g < 14 else (224, 8)
            second = first + gap
        else:
            first = jnp.where(
                g < 8, 8 * g, jnp.where(g < 12, 64 + 8 * g, jnp.where(g < 14, 96 + 8 * g, 224))
            )
            gap = jnp.where(g < 8, 64, jnp.where(g < 12, 32, jnp.where(g < 14, 16, 8)))
            first = pl.multiple_of(first, 8)
            second = pl.multiple_of(first + gap, 8)
        paired(
            to,
            8,
            lambda j: edges[pl.ds(first, 8), lanes(j)],
            lambda j: edges[pl.ds(second, 8), lanes(j)],
        )

    def step(h):
        odd = min(2 * h + 1, 14) if isinstance(h, int) else jnp.minimum(2 * h + 1, 14)
        layout(2 * h, stage)
        if not (isinstance(h, int) and h == 7):
            layout(odd, stage_two)
        for i in range(8):
            keep(stage, i, 16 * h + i)
        if not (isinstance(h, int) and h == 7):
            for i in range(8):
                keep(stage_two, i, 8 * odd + i)

    def last():
        last_levels(edges, stage, stage_two, keep)

    return step, last


def last_levels(edges, stage, stage_two, keep):
    paired(
        stage,
        8,
        lambda j: edges[240:248, lanes(j)],
        lambda j: pltpu.roll(edges[240:248, lanes(j)], 4, 0),
    )
    rows = lax.broadcasted_iota(jnp.int32, (8, 128), 0)

    def last_second(j):
        tile = edges[246:254, lanes(j)]
        return jnp.where(rows < 6, pltpu.roll(tile, 6, 0), pltpu.roll(tile, 7, 0))

    paired(stage_two, 8, lambda j: edges[246:254, lanes(j)], last_second)
    for i in range(4):
        keep(stage, i, 120 + i)
    keep(stage_two, 2, 124)
    keep(stage_two, 3, 125)
    keep(stage_two, 6, 126)


def relayout_edges(edges, stage, stage_two, highs, lows):
    step, last = edge_steps(edges, stage, stage_two, highs, lows)

    def body(h, _):
        step(h)
        return 0

    lax.fori_loop(0, 8, body, 0)
    last()


def up_kernel(
    x_ref, top_ref, own_ref, dst_ref, src_hbm, basis_hbm, edges_hbm, pairs_hbm,
    out_ref, done_ref,
    src_ref, tile_ref, basis, edges, pairs, stage, stage_two, stage_three, stage_four, tops, vec_a, vec_b,
    highs, lows, table, tile_at, sems,
):
    basis_copy = pltpu.make_async_copy(basis_hbm, basis, sems.at[0])
    pair_copies = [
        pltpu.make_async_copy(
            pairs_hbm.at[pl.ds(128 * c, 128)], pairs.at[pl.ds(128 * c, 128)], sems.at[5 + c]
        )
        for c in range(4)
    ]
    edge_copies = [
        pltpu.make_async_copy(
            edges_hbm.at[pl.ds(0, 128)], edges.at[pl.ds(0, 128)], sems.at[1]
        ),
        pltpu.make_async_copy(
            edges_hbm.at[pl.ds(128, EDGE_ROWS - 128)],
            edges.at[pl.ds(128, EDGE_ROWS - 128)],
            sems.at[2],
        ),
    ]
    source_copy = pltpu.make_async_copy(src_hbm, src_ref, sems.at[3])
    tile_copy = pltpu.make_async_copy(tile_at, tile_ref, sems.at[4])
    basis_copy.start()
    source_copy.start()
    for copy in (
        pair_copies[0], edge_copies[0], pair_copies[1], edge_copies[1], pair_copies[2],
        pair_copies[3],
    ):
        copy.start()
    low16, high16 = half_masks(16)
    low = low_lanes(16)

    def clear(i, _):
        out_ref[pl.ds(i * 32, 32)] = jnp.zeros((32, 8, 128), bf16)
        return 0

    lax.fori_loop(0, PEERS * TILES // 32, clear, 0)

    blocks = PAIR_ROWS // 128
    sub = lax.broadcasted_iota(jnp.int32, (128, 128), 0)
    lane = lax.broadcasted_iota(jnp.int32, (128, 128), 1)
    across = [
        jnp.broadcast_to(own_ref[b : b + 1, :].astype(f32), (128, 128)) for b in range(blocks)
    ]
    along = [value.T for value in across]
    wanted = jnp.concatenate(
        [
            jnp.where(
                jnp.broadcast_to(dst_ref[b : b + 1, :].astype(f32), (128, 128)).T
                == lane.astype(f32),
                1.0,
                0.0,
            )
            for b in range(blocks)
        ],
        axis=0,
    ).astype(bf16)
    slots = []
    for c in range(blocks):
        same = jnp.where((along[c] == across[c]) & (sub < lane), 1.0, 0.0)
        for b in range(c):
            same = same + jnp.where(along[b] == across[c], 1.0, 0.0)
        rank = jnp.sum(same, axis=0, keepdims=True)
        tile_at[c : c + 1, :] = (across[c][0:1] * TILES + rank).astype(jnp.int32)
        slots.append(jnp.broadcast_to(across[c][0:1] * SLOTS + rank, (128, 128)))
    tile_copy.start()
    for m in range(SLOTS):
        here = (sub + 128 * m).astype(f32)
        placing = jnp.concatenate(
            [jnp.where(slot == here, 1.0, 0.0) for slot in slots], axis=1
        ).astype(bf16)
        rows = mm(placing, wanted)
        for k in range(16):
            out_ref[(16 * m + k) * TILES + SLOTS + 1] = rows[8 * k : 8 * k + 8].astype(bf16)

    for level in range(LEVELS - 1):
        tile = top_ref[32 * level : 32 * level + 32, :]
        tops[pl.ds(64 * level, 32, stride=2), :] = tile
        tops[pl.ds(64 * level + 1, 32, stride=2), :] = swap(tile)

    basis_copy.wait()

    def leaf_layout(g, to):
        first = pl.multiple_of(16 * g, 16)
        second = pl.multiple_of(64 + 16 * g, 16)
        paired_half(
            to,
            lambda j: basis[pl.ds(first, 16), lanes(j)],
            lambda j: basis[pl.ds(second, 16), lanes(j)],
        )

    def leaf_products(g, at_stage):
        for i in range(0, 16, 2):
            weight = jnp.concatenate([matrix(at_stage, 16, i), matrix(at_stage, 16, i + 1)], axis=0)
            at = pl.multiple_of(g * 1024 + i * 64, 128)
            left = x_ref[:, pl.ds(at, 128)]
            right = x_ref[:, pl.ds(pl.multiple_of(at + FLAT, 128), 128)]
            stacked = jnp.concatenate(
                [left * low16, right * low16, left * high16, right * high16], axis=0
            )
            found = mm(stacked, weight.astype(bf16))
            for k in range(2):
                pair = jnp.where(low, found[32 * k : 32 * k + 16], found[32 * k + 16 : 32 * k + 32])
                turned = swap(pair)
                t = 16 * g + i + k
                vec_a[t] = pair
                table[t] = jnp.where(low, pair, turned).astype(bf16)
                table[t + 64] = jnp.where(low, turned, pair).astype(bf16)

    def leaf_step(h, _):
        leaf_layout(2 * h, stage)
        leaf_layout(2 * h + 1, stage_two)
        leaf_products(2 * h, stage)
        leaf_products(2 * h + 1, stage_two)
        return 0

    lax.fori_loop(0, 2, leaf_step, 0)

    edge_step, edge_last = edge_steps(edges, stage_three, stage_four, highs, lows)

    def parents(nodes, first, amount):
        up = nodes in (128, 32, 8)
        here, there = (vec_a, vec_b) if up else (vec_b, vec_a)
        base = LEVEL_BASE[nodes]
        for k in range(amount):
            q = first + k
            p0 = here[2 * q]
            p1 = here[2 * q + 1]
            both = jnp.concatenate(
                [jnp.where(low, p0, swap(p1)), jnp.where(low, swap(p0), p1)], axis=0
            )
            vh, vl = split(both)
            wh = highs[pl.ds(base + 2 * q, 2)].reshape(128, 128)
            wl = lows[pl.ds(base + 2 * q, 2)].reshape(128, 128)
            two = mm(jnp.concatenate([vh, vl], axis=0), wh)
            found = two[:32] + two[32:] + mm(vh, wl)
            there[q] = jnp.where(low, found[:16], found[16:])

    def root():
        last = vec_a[0]
        both = jnp.concatenate([last, swap(last)], axis=0)[:, :HALF]
        vh, vl = split(both)
        two = mm(jnp.concatenate([vh, vl], axis=0), highs[126])
        found = two[:32] + two[32:] + mm(vh, lows[126])
        return found[:16] + swap(found[16:])

    def carried(current, level):
        wh, wl = split(tops[64 * level : 64 * level + 64, :])
        vh, vl = split(current[:, :HALF])
        two = mm(jnp.concatenate([vh, vl], axis=0), wh)
        return two[:16] + two[16:] + mm(vh, wl)

    me = lax.axis_index("leaf").astype(jnp.int32)

    def send(current, level):
        tile = join(current[0:8], current[8:16]).astype(bf16)
        for x in range(2**level, 2 ** (level + 1)):
            out_ref[lax.bitwise_xor(me, x) * TILES + SLOTS] = tile

    source_copy.wait()
    tile_copy.wait()
    pair_copies[0].wait()

    def pair_layout(g, to):
        first = pl.multiple_of(32 * g, 16)
        second = pl.multiple_of(32 * g + 16, 16)
        paired_half(
            to,
            lambda j: pairs[pl.ds(first, 16), lanes(j)],
            lambda j: pairs[pl.ds(second, 16), lanes(j)],
        )

    def pair_products(g, at):
        zero = jnp.zeros((32, 128), bf16)
        row = g // 4
        column = 32 * (g % 4)
        for i in range(0, 16, 2):
            weight = jnp.concatenate(
                [matrix(at, 16, i), matrix(at, 16, i + 1)], axis=1
            ).astype(bf16)
            listed = [32 * g + i, 32 * g + 16 + i, 32 * g + i + 1, 32 * g + 17 + i]
            sources = [table[src_ref[r]] for r in listed]
            first = jnp.concatenate([sources[0] * low16, sources[1] * high16], axis=0)
            second = jnp.concatenate([sources[2] * low16, sources[3] * high16], axis=0)
            stacked = jnp.concatenate(
                [
                    jnp.concatenate([first, zero], axis=1),
                    jnp.concatenate([zero, second], axis=1),
                ],
                axis=0,
            )
            found = mmt(stacked, weight)
            for k in range(4):
                tile = jnp.concatenate(
                    [found[16 * k : 16 * k + 8], found[16 * k + 8 : 16 * k + 16]], axis=1
                )
                out_ref[tile_ref[row, column + listed[k] - 32 * g]] = tile.astype(bf16)

    groups = PAIR_ROWS // 32
    pair_layout(0, stage)

    def pair_step(h):
        pair_layout(2 * h + 1, stage_two)
        pair_products(2 * h, stage)
        if 2 * h + 2 < groups:
            pair_layout(2 * h + 2, stage)
        pair_products(2 * h + 1, stage_two)

    edge_copies[0].wait()
    edge_step(0)
    edge_step(1)
    pair_step(0)
    pair_copies[1].wait()
    edge_step(2)
    edge_step(3)
    parents(128, 0, 16)
    pair_step(1)
    edge_copies[1].wait()
    edge_step(4)
    edge_step(5)
    parents(128, 16, 16)
    pair_step(2)
    pair_copies[2].wait()
    edge_step(6)
    edge_step(7)
    edge_last()
    parents(64, 0, 16)
    pair_step(3)
    parents(32, 0, 8)
    parents(16, 0, 4)
    pair_step(4)
    pair_copies[3].wait()
    parents(8, 0, 2)
    parents(4, 0, 1)
    current = root()
    send(current, 0)
    current = carried(current, 0)
    pair_step(5)
    for level in range(1, 3):
        send(current, level)
        current = carried(current, level)
    pair_step(6)
    for level in range(3, LEVELS):
        send(current, level)
        if level < LEVELS - 1:
            current = carried(current, level)
    pair_step(7)
    done_ref[...] = current[0:8]


def mid_kernel(
    after_ref, xs_ref, xe_ref, near_hbm, basis_hbm, edges_hbm, top_ref, couple_ref,
    near_ref, down_ref, basis_ref, top_out_ref, ends_ref,
    near, basis, edges, stage, stage_two, vec_a, vec_b, highs, lows, sems,
):
    copies = [
        pltpu.make_async_copy(near_hbm, near, sems.at[0]),
        pltpu.make_async_copy(basis_hbm, basis, sems.at[1]),
        pltpu.make_async_copy(edges_hbm, edges, sems.at[2]),
    ]
    for copy in copies:
        copy.start()
    low16, _ = half_masks(16)
    low64, high64 = half_masks(64)

    copies[0].wait()

    def near_group(g, _):
        first = pl.multiple_of(16 * g, 16)
        rows = pl.ds(first, 16)
        paired(
            stage,
            16,
            lambda j: near[rows, lanes(j)].astype(f32),
            lambda j: near[rows, lanes(j, FLAT)].astype(f32),
        )
        for j in range(32):
            tile = near[rows, lanes(j, 2 * FLAT)].astype(f32)
            stage_two[pl.ds(32 * j, 16), :] = tile
            stage_two[pl.ds(32 * j + 16, 16), :] = swap(tile)
        for i in range(0, 16, 2):
            at = pl.multiple_of(g * 1024 + i * 64, 128)
            after = pl.multiple_of(at + 128, 128)
            found = []
            for k, ref in enumerate((xs_ref, xe_ref)):
                weight = jnp.concatenate(
                    [matrix(stage, 16, i + k), matrix(stage_two, 16, i + k)], axis=1
                ).astype(bf16)
                vec = jnp.concatenate(
                    [ref[:, pl.ds(at, 128)], ref[:, pl.ds(after, 128)] * low16], axis=1
                )
                found.append(mmt(vec, weight))
            near_ref[:, pl.ds(at, 128)] = jnp.concatenate(found, axis=1)

        @pl.when(g == 0)
        def _():
            vec_a[0] = matrix(stage, 16, 0)

        return 0

    lax.fori_loop(0, 8, near_group, 0)
    ends_ref[...] = join(vec_a[0], matrix(stage_two, 16, 15)).astype(bf16)

    copies[1].wait()
    wide = low_lanes(64)
    even = (lax.broadcasted_iota(jnp.int32, (16, 128), 0) % 2) == 0

    def basis_group(g, _):
        rows = pl.ds(pl.multiple_of(16 * g, 16), 16)
        for j in range(32):
            tile = basis[rows, lanes(j)].astype(f32)
            turned = swap(tile)
            stage[pl.ds(32 * j, 16), :] = jnp.where(even, tile, turned)
            stage[pl.ds(32 * j + 16, 16), :] = jnp.where(even, turned, tile)
        for i in range(0, 16, 2):
            at = pl.multiple_of(g * 512 + i * 32, 64)
            basis_ref[pl.ds(at, 64), :] = jnp.where(
                wide, matrix(stage, 16, i), matrix(stage, 16, i + 1)
            ).astype(bf16)
        return 0

    lax.fori_loop(0, 8, basis_group, 0)

    copies[2].wait()
    relayout_edges(edges, stage, stage_two, highs, lows)
    vec_a[0] = highs[126].astype(f32) + lows[126].astype(f32)
    here, there = vec_a, vec_b
    nodes = 4
    while nodes <= LEAF_DEV:
        base = LEVEL_BASE[nodes]

        def children(q, here=here, there=there, base=base, final=nodes == LEAF_DEV):
            ph, plow = split(here[q])
            rh = jnp.concatenate([ph * low64, ph * high64], axis=0)
            rl = jnp.concatenate([plow * low64, plow * high64], axis=0)
            wh = highs[pl.ds(base + 2 * q, 2)].reshape(128, 128)
            wl = lows[pl.ds(base + 2 * q, 2)].reshape(128, 128)
            found = mm(wh, rh) + mm(wl, rh) + mm(wh, rl)
            if not final:
                there[2 * q] = found[:64]
                there[2 * q + 1] = found[64:]
            else:
                at = pl.multiple_of(q * 128, 128)
                down_ref[pl.ds(at, 128), :] = found.astype(bf16)

        quarter = nodes // 4
        if quarter > 4:

            def block(i, _, children=children):
                for k in range(4):
                    children(4 * i + k)
                return 0

            lax.fori_loop(0, quarter // 4, block, 0)
        else:
            for q in range(quarter):
                children(q)
        here, there = there, here
        nodes *= 2

    low = low_lanes(64)
    low32 = low_lanes(32)
    for level in range(LEVELS):
        second = couple_ref[32 * level : 32 * level + 32, :]
        first = top_ref[32 * level : 32 * level + 32, :] if level < LEVELS - 1 else second
        stage[pl.ds(64 * level, 32, stride=2), :] = jnp.where(low32, first, swap(second))
        stage[pl.ds(64 * level + 1, 32, stride=2), :] = jnp.where(low32, swap(first), second)
    chain = None
    for level in range(LEVELS):
        value = stage[64 * level : 64 * level + 64, :]
        if chain is None:
            found = value
        else:
            wh, wl = split(value)
            vh, vl = split(chain[:, :HALF])
            found = mm(vh, wh) + mm(vl, wh) + mm(vh, wl)
        chain = found
        high = found.astype(bf16).astype(f32)
        top_out_ref[level] = jnp.where(low, swap(high), found - high).astype(bf16)


def down_kernel(
    got_hbm, near_hbm, down_hbm, basis_hbm, top_ref, ends_ref, before_ref, following_ref,
    out_ref,
    got, near, down, basis, values, target, far, sems,
):
    span = PEERS // CHUNKS
    arriving = [
        pltpu.make_async_copy(
            got_hbm.at[pl.ds(c * span * TILES, span * TILES)],
            got.at[pl.ds(c * span * TILES, span * TILES)],
            sems.at[c],
        )
        for c in range(CHUNKS)
    ]
    copies = [
        pltpu.make_async_copy(down_hbm, down, sems.at[CHUNKS]),
        pltpu.make_async_copy(basis_hbm, basis, sems.at[CHUNKS + 1]),
        pltpu.make_async_copy(near_hbm, near, sems.at[CHUNKS + 2]),
    ]
    for copy in arriving:
        copy.start()
    low8 = low_lanes(8)
    low16, high16 = half_masks(16)

    def unpack(o, _):
        for s in range(SLOTS):
            at = pl.multiple_of((o * SLOTS + s) * 8, 8)
            values[pl.ds(at, 8), :] = got[o * TILES + s].astype(f32)
        at = pl.multiple_of(o * SLOTS, 8)
        target[pl.ds(at, 8), :] = got[o * TILES + SLOTS + 1].astype(f32)
        return 0

    for c in range(CHUNKS):
        arriving[c].wait()
        if c == 0:
            for copy in copies:
                copy.start()
        lax.fori_loop(c * span, (c + 1) * span, unpack, 0, unroll=8)
    landing = jnp.concatenate(
        [target[128 * i : 128 * i + 128, :].T for i in range(SLOTS)], axis=1
    ).astype(bf16)
    for u in range(0, 8, 2):
        chosen = jnp.concatenate(
            [values[pl.ds(u + k, PEERS * SLOTS, stride=8), :] for k in range(2)], axis=1
        ).astype(bf16)
        found = mm(landing, chosen)
        far[128 * u : 128 * u + 128, :] = found[:, :128]
        far[128 * u + 128 : 128 * u + 256, :] = found[:, 128:]

    def doubled(tile):
        turned = swap(tile)
        return jnp.concatenate(
            [jnp.where(low8, tile, turned), jnp.where(low8, turned, tile)], axis=0
        )

    me = lax.axis_index("leaf").astype(jnp.int32)
    total = jnp.zeros((2 * NV, HALF), f32)
    for level in range(LEVELS):
        parts = []
        for x in range(2**level, 2 ** (level + 1)):
            tile = got[lax.bitwise_xor(me, x) * TILES + SLOTS].astype(f32)
            if len(parts) < 4:
                parts.append(tile)
            else:
                parts[x % 4] = parts[x % 4] + tile
        tile = parts[0]
        for part in parts[1:]:
            tile = tile + part
        high, rest = split(doubled(tile))
        total = total + mmt(jnp.concatenate([high, rest * low16], axis=0), top_ref[level])
    root = total[:NV] + total[NV:]
    high, rest = split(jnp.concatenate([root, root], axis=1))
    root = jnp.concatenate([high * low16, high * high16, rest * low16, rest * high16], axis=0)

    for copy in copies:
        copy.wait()
    zero = jnp.zeros((2 * NV, 128), bf16)
    for c in range(8):
        found = mmt(root, down[512 * c : 512 * c + 512, :])
        for half in range(2):
            block = found[16 * half : 16 * half + 16] + found[32 + 16 * half : 48 + 16 * half]
            pieces = []
            for k in range(4):
                leaf = 64 * half + 8 * c + 2 * k
                f0 = far[pl.ds(leaf, 8, stride=128), :]
                f1 = far[pl.ds(leaf + 1, 8, stride=128), :]
                gathered = jnp.concatenate(
                    [jnp.where(low8, f0, swap(f1)), jnp.where(low8, swap(f0), f1)], axis=0
                )
                hat = (block[:, 128 * k : 128 * k + 128] + gathered).astype(bf16)
                pieces.append(jnp.concatenate([hat * low16, hat * high16], axis=0))
            for k in range(0, 4, 2):
                leaf = 64 * half + 8 * c + 2 * k
                stacked = jnp.concatenate(
                    [
                        jnp.concatenate([pieces[k], zero], axis=1),
                        jnp.concatenate([zero, pieces[k + 1]], axis=1),
                    ],
                    axis=0,
                )
                weight = jnp.concatenate(
                    [
                        basis[32 * leaf : 32 * leaf + 64, :],
                        basis[32 * leaf + 64 : 32 * leaf + 128, :],
                    ],
                    axis=1,
                )
                part = mmt(stacked, weight)
                for m in range(2):
                    at = 64 * leaf + 128 * m
                    out_ref[:, at : at + 128] = (
                        jnp.concatenate(
                            [part[32 * m : 32 * m + 16], part[32 * m + 16 : 32 * m + 32]], axis=1
                        )
                        + near[:, at : at + 128]
                    )
    edge = jnp.zeros((NV, HALF), f32)
    out_ref[:, :128] += jnp.concatenate([mmt(before_ref[...], ends_ref[:, :HALF]), edge], axis=1)
    out_ref[:, 8064:] += jnp.concatenate(
        [edge, mmt(following_ref[...], ends_ref[:, HALF:])], axis=1
    )


def vmem():
    return pl.BlockSpec(memory_space=pltpu.VMEM)


def hbm():
    return pl.BlockSpec(memory_space=pltpu.HBM)


def params(mib):
    return pltpu.CompilerParams(vmem_limit_bytes=mib * MIB)


def shape(dims, dtype):
    return jax.ShapeDtypeStruct(dims, dtype)


def run_up(src, own, dst, x_vecs, basis, edges, top_edges, pairs):
    return pl.pallas_call(
        up_kernel,
        name="up",
        out_shape=(shape((PEERS * TILES, 8, 128), bf16), shape((8, 128), f32)),
        in_specs=[vmem(), vmem(), vmem(), vmem(), hbm(), hbm(), hbm(), hbm()],
        out_specs=(vmem(), vmem()),
        scratch_shapes=[
            pltpu.SMEM((PAIR_ROWS,), jnp.int32),
            pltpu.SMEM((PAIR_ROWS // 128, 128), jnp.int32),
            pltpu.VMEM((LEAF_DEV, FLAT), bf16),
            pltpu.VMEM((EDGE_ROWS, FLAT), f32),
            pltpu.VMEM((PAIR_ROWS, FLAT), bf16),
            pltpu.VMEM((1024, 128), f32),
            pltpu.VMEM((1024, 128), f32),
            pltpu.VMEM((512, 128), f32),
            pltpu.VMEM((512, 128), f32),
            pltpu.VMEM((64 * (LEVELS - 1), 128), f32),
            pltpu.VMEM((64, NV, 128), f32),
            pltpu.VMEM((64, NV, 128), f32),
            pltpu.VMEM((128, 64, 128), bf16),
            pltpu.VMEM((128, 64, 128), bf16),
            pltpu.VMEM((LEAF_DEV, NV, 128), bf16),
            pltpu.VMEM((PAIR_ROWS // 128, 128), jnp.int32),
            pltpu.SemaphoreType.DMA((9,)),
        ],
        compiler_params=params(60),
        cost_estimate=pl.CostEstimate(
            flops=10**9, bytes_accessed=12 * 10**6, transcendentals=0
        ),
    )(x_vecs, top_edges, own, dst, src, basis, edges, pairs)


def run_mid(after, xs, xe, near, basis, edges, top, couple):
    return pl.pallas_call(
        mid_kernel,
        name="mid",
        out_shape=(
            shape((NV, LEAF_DEV * LEAF), f32),
            shape((LEAF_DEV * RANK // 2, 128), bf16),
            shape((LEAF_DEV * LEAF // 2, 128), bf16),
            shape((LEVELS, RANK, 128), bf16),
            shape((LEAF, 128), bf16),
        ),
        in_specs=[vmem(), vmem(), vmem(), hbm(), hbm(), hbm(), vmem(), vmem()],
        out_specs=(vmem(), vmem(), vmem(), vmem(), vmem()),
        scratch_shapes=[
            pltpu.VMEM((LEAF_DEV, 3 * FLAT), bf16),
            pltpu.VMEM((LEAF_DEV, FLAT), bf16),
            pltpu.VMEM((EDGE_ROWS, FLAT), f32),
            pltpu.VMEM((1024, 128), f32),
            pltpu.VMEM((1024, 128), f32),
            pltpu.VMEM((64, 64, 128), f32),
            pltpu.VMEM((64, 64, 128), f32),
            pltpu.VMEM((128, 64, 128), bf16),
            pltpu.VMEM((128, 64, 128), bf16),
            pltpu.SemaphoreType.DMA((3,)),
        ],
        compiler_params=params(62),
        cost_estimate=pl.CostEstimate(
            flops=10**9, bytes_accessed=14 * 10**6, transcendentals=0
        ),
    )(after, xs, xe, near, basis, edges, top, couple)


def run_down(got, near, down, basis, top, ends, before, following):
    return pl.pallas_call(
        down_kernel,
        name="down",
        out_shape=shape((NV, LEAF_DEV * LEAF), f32),
        in_specs=[hbm(), hbm(), hbm(), hbm(), vmem(), vmem(), vmem(), vmem()],
        out_specs=vmem(),
        scratch_shapes=[
            pltpu.VMEM((PEERS * TILES, 8, 128), bf16),
            pltpu.VMEM((NV, LEAF_DEV * LEAF), f32),
            pltpu.VMEM((LEAF_DEV * RANK // 2, 128), bf16),
            pltpu.VMEM((LEAF_DEV * LEAF // 2, 128), bf16),
            pltpu.VMEM((PEERS * SLOTS * 8, 128), f32),
            pltpu.VMEM((PEERS * SLOTS, 128), f32),
            pltpu.VMEM((8 * LEAF_DEV, 128), f32),
            pltpu.SemaphoreType.DMA((CHUNKS + 3,)),
        ],
        compiler_params=params(59),
        cost_estimate=pl.CostEstimate(
            flops=10**9, bytes_accessed=8 * 10**6, transcendentals=0
        ),
    )(got, near, down, basis, top, ends, before, following)


def shards(
    x_vecs,
    leaf_basis,
    near_blocks,
    local_edges,
    top_edges,
    top_couple,
    couple_blocks,
    couple_src,
    couple_owner,
    couple_dst,
):
    top_flat = top_edges.reshape((LEVELS - 1) * 32, 128)
    outgoing, after = run_up(
        couple_src, couple_owner.reshape(PAIR_ROWS // 128, 128),
        couple_dst.reshape(PAIR_ROWS // 128, 128), x_vecs, leaf_basis, local_edges, top_flat,
        couple_blocks,
    )
    first, last, after = lax.optimization_barrier((x_vecs[:, :LEAF], x_vecs[:, -LEAF:], after))
    ahead = [(i, (i + 1) % PEERS) for i in range(PEERS)]
    back = [(target, source) for source, target in ahead]
    before = lax.ppermute(last, "leaf", ahead)
    following = lax.ppermute(first, "leaf", back)
    got = lax.all_to_all(
        outgoing.reshape(PEERS, TILES * 8, 128), "leaf", split_axis=0, concat_axis=0, tiled=True
    ).reshape(PEERS * TILES, 8, 128)
    fill = jnp.zeros((NV, LEAF), bf16)
    xs = jnp.concatenate([fill, x_vecs, fill], axis=1)
    xe = jnp.concatenate([x_vecs, fill, fill], axis=1)
    near, down, basis, tops, ends = run_mid(
        after, xs, xe, near_blocks, leaf_basis, local_edges, top_flat,
        top_couple.reshape(LEVELS * 32, 128),
    )
    return run_down(got, near, down, basis, tops, ends, before, following)


def solution(mesh):
    return jax.shard_map(
        shards,
        mesh=mesh,
        in_specs=(
            P(None, "leaf"),
            P("leaf", None),
            P("leaf", None),
            P("leaf", None),
            P("leaf", None, None),
            P("leaf", None, None),
            P("leaf", None),
            P("leaf"),
            P("leaf", None),
            P("leaf"),
        ),
        out_specs=P(None, "leaf"),
        check_vma=False,
    )
```

```python
import jax
import jax.numpy as jnp
from jax import lax
from jax.experimental import pallas as pl
from jax.experimental.pallas import tpu as pltpu
from jax.sharding import PartitionSpec as P

LEAF = 64
RANK = 64
NV = 16
LEAF_DEV = 128
PEERS = 128
LEVELS = 7
SLOTS = 8
TILES = SLOTS + 2
PAIR_ROWS = 512
CHUNKS = 4
EDGE_ROWS = 254
FLAT = 4096
HALF = 64
MIB = 1024 * 1024

LEVEL_BASE = {128: 0, 64: 64, 32: 96, 16: 112, 8: 120, 4: 124, 2: 126}

f32 = jnp.float32
bf16 = jnp.bfloat16


def low_lanes(rows):
    return lax.broadcasted_iota(jnp.int32, (rows, 128), 1) < HALF


def half_masks(rows):
    low = low_lanes(rows).astype(f32)
    return low.astype(bf16), (1.0 - low).astype(bf16)


def swap(value):
    return pltpu.roll(value, HALF, 1)


def join(first, second):
    return jnp.where(low_lanes(first.shape[0]), first, swap(second))


def split(value):
    high = value.astype(bf16)
    return high, (value - high.astype(f32)).astype(bf16)


def mm(left, right):
    return jnp.dot(left, right, preferred_element_type=f32)


def mmt(left, right):
    return lax.dot_general(left, right, (((1,), (1,)), ((), ())), preferred_element_type=f32)


def paired(stage, group, load_first, load_second):
    low = low_lanes(group)
    for j in range(32):
        first = load_first(j)
        second = load_second(j)
        stage[pl.ds(2 * j * group, group), :] = jnp.where(low, first, swap(second))
        stage[pl.ds((2 * j + 1) * group, group), :] = jnp.where(low, swap(first), second)


def paired_half(stage, load_first, load_second):
    for j in range(32):
        first = load_first(j)
        second = load_second(j)
        stage[pl.ds(32 * j, 16), :] = jnp.concatenate(
            [first[:, :HALF], second[:, :HALF]], axis=1
        ).astype(f32)
        stage[pl.ds(32 * j + 16, 16), :] = jnp.concatenate(
            [first[:, HALF:], second[:, HALF:]], axis=1
        ).astype(f32)


def matrix(stage, group, index):
    return stage[pl.ds(index, 64, stride=group), :]


def lanes(j, start=0):
    return pl.ds(start + j * 128, 128)


def edge_steps(edges, stage, stage_two, highs, lows):
    def keep(at, index, place):
        high, low = split(matrix(at, 8, index))
        highs[place] = high
        lows[place] = low

    def layout(g, to):
        if isinstance(g, int):
            first, gap = 8 * g, 64
            if g >= 8:
                first, gap = (64 + 8 * g, 32) if g < 12 else (96 + 8 * g, 16) if g < 14 else (224, 8)
            second = first + gap
        else:
            first = jnp.where(
                g < 8, 8 * g, jnp.where(g < 12, 64 + 8 * g, jnp.where(g < 14, 96 + 8 * g, 224))
            )
            gap = jnp.where(g < 8, 64, jnp.where(g < 12, 32, jnp.where(g < 14, 16, 8)))
            first = pl.multiple_of(first, 8)
            second = pl.multiple_of(first + gap, 8)
        paired(
            to,
            8,
            lambda j: edges[pl.ds(first, 8), lanes(j)],
            lambda j: edges[pl.ds(second, 8), lanes(j)],
        )

    def step(h):
        odd = min(2 * h + 1, 14) if isinstance(h, int) else jnp.minimum(2 * h + 1, 14)
        layout(2 * h, stage)
        if not (isinstance(h, int) and h == 7):
            layout(odd, stage_two)
        for i in range(8):
            keep(stage, i, 16 * h + i)
        if not (isinstance(h, int) and h == 7):
            for i in range(8):
                keep(stage_two, i, 8 * odd + i)

    def last():
        last_levels(edges, stage, stage_two, keep)

    return step, last


def last_levels(edges, stage, stage_two, keep):
    paired(
        stage,
        8,
        lambda j: edges[240:248, lanes(j)],
        lambda j: pltpu.roll(edges[240:248, lanes(j)], 4, 0),
    )
    rows = lax.broadcasted_iota(jnp.int32, (8, 128), 0)

    def last_second(j):
        tile = edges[246:254, lanes(j)]
        return jnp.where(rows < 6, pltpu.roll(tile, 6, 0), pltpu.roll(tile, 7, 0))

    paired(stage_two, 8, lambda j: edges[246:254, lanes(j)], last_second)
    for i in range(4):
        keep(stage, i, 120 + i)
    keep(stage_two, 2, 124)
    keep(stage_two, 3, 125)
    keep(stage_two, 6, 126)


def relayout_edges(edges, stage, stage_two, highs, lows):
    step, last = edge_steps(edges, stage, stage_two, highs, lows)

    def body(h, _):
        step(h)
        return 0

    lax.fori_loop(0, 8, body, 0)
    last()


def up_kernel(
    x_ref, top_ref, own_ref, dst_ref, src_hbm, basis_hbm, edges_hbm, pairs_hbm,
    out_ref, done_ref,
    src_ref, tile_ref, basis, edges, pairs, stage, stage_two, stage_three, stage_four, tops, vec_a, vec_b,
    highs, lows, table, tile_at, sems,
):
    basis_copy = pltpu.make_async_copy(basis_hbm, basis, sems.at[0])
    pair_copies = [
        pltpu.make_async_copy(
            pairs_hbm.at[pl.ds(128 * c, 128)], pairs.at[pl.ds(128 * c, 128)], sems.at[5 + c]
        )
        for c in range(4)
    ]
    edge_copies = [
        pltpu.make_async_copy(
            edges_hbm.at[pl.ds(0, 128)], edges.at[pl.ds(0, 128)], sems.at[1]
        ),
        pltpu.make_async_copy(
            edges_hbm.at[pl.ds(128, EDGE_ROWS - 128)],
            edges.at[pl.ds(128, EDGE_ROWS - 128)],
            sems.at[2],
        ),
    ]
    source_copy = pltpu.make_async_copy(src_hbm, src_ref, sems.at[3])
    tile_copy = pltpu.make_async_copy(tile_at, tile_ref, sems.at[4])
    basis_copy.start()
    source_copy.start()
    for copy in (
        pair_copies[0], edge_copies[0], pair_copies[1], edge_copies[1], pair_copies[2],
        pair_copies[3],
    ):
        copy.start()
    low16, high16 = half_masks(16)
    low = low_lanes(16)

    def clear(i, _):
        out_ref[pl.ds(i * 32, 32)] = jnp.zeros((32, 8, 128), bf16)
        return 0

    lax.fori_loop(0, PEERS * TILES // 32, clear, 0)

    blocks = PAIR_ROWS // 128
    sub = lax.broadcasted_iota(jnp.int32, (128, 128), 0)
    lane = lax.broadcasted_iota(jnp.int32, (128, 128), 1)
    across = [
        jnp.broadcast_to(own_ref[b : b + 1, :].astype(f32), (128, 128)) for b in range(blocks)
    ]
    along = [value.T for value in across]
    wanted = jnp.concatenate(
        [
            jnp.where(
                jnp.broadcast_to(dst_ref[b : b + 1, :].astype(f32), (128, 128)).T
                == lane.astype(f32),
                1.0,
                0.0,
            )
            for b in range(blocks)
        ],
        axis=0,
    ).astype(bf16)
    slots = []
    for c in range(blocks):
        same = jnp.where((along[c] == across[c]) & (sub < lane), 1.0, 0.0)
        for b in range(c):
            same = same + jnp.where(along[b] == across[c], 1.0, 0.0)
        rank = jnp.sum(same, axis=0, keepdims=True)
        tile_at[c : c + 1, :] = (across[c][0:1] * TILES + rank).astype(jnp.int32)
        slots.append(jnp.broadcast_to(across[c][0:1] * SLOTS + rank, (128, 128)))
    tile_copy.start()
    for m in range(SLOTS):
        here = (sub + 128 * m).astype(f32)
        placing = jnp.concatenate(
            [jnp.where(slot == here, 1.0, 0.0) for slot in slots], axis=1
        ).astype(bf16)
        rows = mm(placing, wanted)
        for k in range(16):
            out_ref[(16 * m + k) * TILES + SLOTS + 1] = rows[8 * k : 8 * k + 8].astype(bf16)

    for level in range(LEVELS - 1):
        tile = top_ref[32 * level : 32 * level + 32, :]
        tops[pl.ds(64 * level, 32, stride=2), :] = tile
        tops[pl.ds(64 * level + 1, 32, stride=2), :] = swap(tile)

    basis_copy.wait()

    def leaf_layout(g, to):
        first = pl.multiple_of(16 * g, 16)
        second = pl.multiple_of(64 + 16 * g, 16)
        paired_half(
            to,
            lambda j: basis[pl.ds(first, 16), lanes(j)],
            lambda j: basis[pl.ds(second, 16), lanes(j)],
        )

    def leaf_products(g, at_stage):
        for i in range(0, 16, 2):
            weight = jnp.concatenate([matrix(at_stage, 16, i), matrix(at_stage, 16, i + 1)], axis=0)
            at = pl.multiple_of(g * 1024 + i * 64, 128)
            left = x_ref[:, pl.ds(at, 128)]
            right = x_ref[:, pl.ds(pl.multiple_of(at + FLAT, 128), 128)]
            stacked = jnp.concatenate(
                [left * low16, right * low16, left * high16, right * high16], axis=0
            )
            found = mm(stacked, weight.astype(bf16))
            for k in range(2):
                pair = jnp.where(low, found[32 * k : 32 * k + 16], found[32 * k + 16 : 32 * k + 32])
                turned = swap(pair)
                t = 16 * g + i + k
                vec_a[t] = pair
                table[t] = jnp.where(low, pair, turned).astype(bf16)
                table[t + 64] = jnp.where(low, turned, pair).astype(bf16)

    def leaf_step(h):
        leaf_layout(2 * h, stage)
        leaf_layout(2 * h + 1, stage_two)
        leaf_products(2 * h, stage)
        leaf_products(2 * h + 1, stage_two)

    leaf_step(0)
    leaf_step(1)

    edge_step, edge_last = edge_steps(edges, stage_three, stage_four, highs, lows)

    def parents(nodes, first, amount):
        up = nodes in (128, 32, 8)
        here, there = (vec_a, vec_b) if up else (vec_b, vec_a)
        base = LEVEL_BASE[nodes]
        for k in range(amount):
            q = first + k
            p0 = here[2 * q]
            p1 = here[2 * q + 1]
            both = jnp.concatenate(
                [jnp.where(low, p0, swap(p1)), jnp.where(low, swap(p0), p1)], axis=0
            )
            vh, vl = split(both)
            wh = highs[pl.ds(base + 2 * q, 2)].reshape(128, 128)
            wl = lows[pl.ds(base + 2 * q, 2)].reshape(128, 128)
            two = mm(jnp.concatenate([vh, vl], axis=0), wh)
            found = two[:32] + two[32:] + mm(vh, wl)
            there[q] = jnp.where(low, found[:16], found[16:])

    def root():
        last = vec_a[0]
        both = jnp.concatenate([last, swap(last)], axis=0)[:, :HALF]
        vh, vl = split(both)
        two = mm(jnp.concatenate([vh, vl], axis=0), highs[126])
        found = two[:32] + two[32:] + mm(vh, lows[126])
        return found[:16] + swap(found[16:])

    def carried(current, level):
        wh, wl = split(tops[64 * level : 64 * level + 64, :])
        vh, vl = split(current[:, :HALF])
        two = mm(jnp.concatenate([vh, vl], axis=0), wh)
        return two[:16] + two[16:] + mm(vh, wl)

    me = lax.axis_index("leaf").astype(jnp.int32)

    def send(current, level):
        tile = join(current[0:8], current[8:16]).astype(bf16)
        for x in range(2**level, 2 ** (level + 1)):
            out_ref[lax.bitwise_xor(me, x) * TILES + SLOTS] = tile

    source_copy.wait()
    tile_copy.wait()
    pair_copies[0].wait()

    def pair_layout(g, to):
        first = pl.multiple_of(32 * g, 16)
        second = pl.multiple_of(32 * g + 16, 16)
        paired_half(
            to,
            lambda j: pairs[pl.ds(first, 16), lanes(j)],
            lambda j: pairs[pl.ds(second, 16), lanes(j)],
        )

    def pair_products(g, at):
        zero = jnp.zeros((32, 128), bf16)
        row = g // 4
        column = 32 * (g % 4)
        for i in range(0, 16, 2):
            weight = jnp.concatenate(
                [matrix(at, 16, i), matrix(at, 16, i + 1)], axis=1
            ).astype(bf16)
            listed = [32 * g + i, 32 * g + 16 + i, 32 * g + i + 1, 32 * g + 17 + i]
            sources = [table[src_ref[r]] for r in listed]
            first = jnp.concatenate([sources[0] * low16, sources[1] * high16], axis=0)
            second = jnp.concatenate([sources[2] * low16, sources[3] * high16], axis=0)
            stacked = jnp.concatenate(
                [
                    jnp.concatenate([first, zero], axis=1),
                    jnp.concatenate([zero, second], axis=1),
                ],
                axis=0,
            )
            found = mmt(stacked, weight)
            for k in range(4):
                tile = jnp.concatenate(
                    [found[16 * k : 16 * k + 8], found[16 * k + 8 : 16 * k + 16]], axis=1
                )
                out_ref[tile_ref[row, column + listed[k] - 32 * g]] = tile.astype(bf16)

    groups = PAIR_ROWS // 32
    pair_layout(0, stage)

    def pair_step(h):
        pair_layout(2 * h + 1, stage_two)
        pair_products(2 * h, stage)
        if 2 * h + 2 < groups:
            pair_layout(2 * h + 2, stage)
        pair_products(2 * h + 1, stage_two)

    edge_copies[0].wait()
    edge_step(0)
    edge_step(1)
    pair_step(0)
    pair_copies[1].wait()
    edge_step(2)
    edge_step(3)
    parents(128, 0, 16)
    pair_step(1)
    edge_copies[1].wait()
    edge_step(4)
    edge_step(5)
    parents(128, 16, 16)
    pair_step(2)
    pair_copies[2].wait()
    edge_step(6)
    edge_step(7)
    edge_last()
    parents(64, 0, 16)
    pair_step(3)
    parents(32, 0, 8)
    parents(16, 0, 4)
    pair_step(4)
    pair_copies[3].wait()
    parents(8, 0, 2)
    parents(4, 0, 1)
    current = root()
    send(current, 0)
    current = carried(current, 0)
    pair_step(5)
    for level in range(1, 3):
        send(current, level)
        current = carried(current, level)
    pair_step(6)
    for level in range(3, LEVELS):
        send(current, level)
        if level < LEVELS - 1:
            current = carried(current, level)
    pair_step(7)
    done_ref[...] = current[0:8]


def mid_kernel(
    after_ref, xs_ref, xe_ref, near_hbm, basis_hbm, edges_hbm, top_ref, couple_ref,
    near_ref, down_ref, basis_ref, top_out_ref, ends_ref,
    near, basis, edges, stage, stage_two, vec_a, vec_b, highs, lows, sems,
):
    copies = [
        pltpu.make_async_copy(near_hbm, near, sems.at[0]),
        pltpu.make_async_copy(basis_hbm, basis, sems.at[1]),
        pltpu.make_async_copy(edges_hbm, edges, sems.at[2]),
    ]
    for copy in copies:
        copy.start()
    low16, _ = half_masks(16)
    low64, high64 = half_masks(64)

    copies[0].wait()

    def near_group(g, _):
        first = pl.multiple_of(16 * g, 16)
        rows = pl.ds(first, 16)
        paired(
            stage,
            16,
            lambda j: near[rows, lanes(j)].astype(f32),
            lambda j: near[rows, lanes(j, FLAT)].astype(f32),
        )
        for j in range(32):
            tile = near[rows, lanes(j, 2 * FLAT)].astype(f32)
            stage_two[pl.ds(32 * j, 16), :] = tile
            stage_two[pl.ds(32 * j + 16, 16), :] = swap(tile)
        for i in range(0, 16, 2):
            at = pl.multiple_of(g * 1024 + i * 64, 128)
            after = pl.multiple_of(at + 128, 128)
            found = []
            for k, ref in enumerate((xs_ref, xe_ref)):
                weight = jnp.concatenate(
                    [matrix(stage, 16, i + k), matrix(stage_two, 16, i + k)], axis=1
                ).astype(bf16)
                vec = jnp.concatenate(
                    [ref[:, pl.ds(at, 128)], ref[:, pl.ds(after, 128)] * low16], axis=1
                )
                found.append(mmt(vec, weight))
            near_ref[:, pl.ds(at, 128)] = jnp.concatenate(found, axis=1)

        @pl.when(g == 0)
        def _():
            vec_a[0] = matrix(stage, 16, 0)

        return 0

    lax.fori_loop(0, 8, near_group, 0)
    ends_ref[...] = join(vec_a[0], matrix(stage_two, 16, 15)).astype(bf16)

    copies[1].wait()
    wide = low_lanes(64)
    even = (lax.broadcasted_iota(jnp.int32, (16, 128), 0) % 2) == 0

    def basis_group(g, _):
        rows = pl.ds(pl.multiple_of(16 * g, 16), 16)
        for j in range(32):
            tile = basis[rows, lanes(j)].astype(f32)
            turned = swap(tile)
            stage[pl.ds(32 * j, 16), :] = jnp.where(even, tile, turned)
            stage[pl.ds(32 * j + 16, 16), :] = jnp.where(even, turned, tile)
        for i in range(0, 16, 2):
            at = pl.multiple_of(g * 512 + i * 32, 64)
            basis_ref[pl.ds(at, 64), :] = jnp.where(
                wide, matrix(stage, 16, i), matrix(stage, 16, i + 1)
            ).astype(bf16)
        return 0

    lax.fori_loop(0, 8, basis_group, 0)

    copies[2].wait()
    relayout_edges(edges, stage, stage_two, highs, lows)
    vec_a[0] = highs[126].astype(f32) + lows[126].astype(f32)
    here, there = vec_a, vec_b
    nodes = 4
    while nodes <= LEAF_DEV:
        base = LEVEL_BASE[nodes]

        def children(q, here=here, there=there, base=base, final=nodes == LEAF_DEV):
            ph, plow = split(here[q])
            rh = jnp.concatenate([ph * low64, ph * high64], axis=0)
            rl = jnp.concatenate([plow * low64, plow * high64], axis=0)
            wh = highs[pl.ds(base + 2 * q, 2)].reshape(128, 128)
            wl = lows[pl.ds(base + 2 * q, 2)].reshape(128, 128)
            found = mm(wh, rh) + mm(wl, rh) + mm(wh, rl)
            if not final:
                there[2 * q] = found[:64]
                there[2 * q + 1] = found[64:]
            else:
                at = pl.multiple_of(q * 128, 128)
                down_ref[pl.ds(at, 128), :] = found.astype(bf16)

        quarter = nodes // 4
        if quarter > 4:

            def block(i, _, children=children):
                for k in range(4):
                    children(4 * i + k)
                return 0

            lax.fori_loop(0, quarter // 4, block, 0)
        else:
            for q in range(quarter):
                children(q)
        here, there = there, here
        nodes *= 2

    low = low_lanes(64)
    low32 = low_lanes(32)
    for level in range(LEVELS):
        second = couple_ref[32 * level : 32 * level + 32, :]
        first = top_ref[32 * level : 32 * level + 32, :] if level < LEVELS - 1 else second
        stage[pl.ds(64 * level, 32, stride=2), :] = jnp.where(low32, first, swap(second))
        stage[pl.ds(64 * level + 1, 32, stride=2), :] = jnp.where(low32, swap(first), second)
    chain = None
    for level in range(LEVELS):
        value = stage[64 * level : 64 * level + 64, :]
        if chain is None:
            found = value
        else:
            wh, wl = split(value)
            vh, vl = split(chain[:, :HALF])
            found = mm(vh, wh) + mm(vl, wh) + mm(vh, wl)
        chain = found
        high = found.astype(bf16).astype(f32)
        top_out_ref[level] = jnp.where(low, swap(high), found - high).astype(bf16)


def down_kernel(
    got_hbm, near_hbm, down_hbm, basis_hbm, top_ref, ends_ref, before_ref, following_ref,
    out_ref,
    got, near, down, basis, values, target, far, sems,
):
    span = PEERS // CHUNKS
    arriving = [
        pltpu.make_async_copy(
            got_hbm.at[pl.ds(c * span * TILES, span * TILES)],
            got.at[pl.ds(c * span * TILES, span * TILES)],
            sems.at[c],
        )
        for c in range(CHUNKS)
    ]
    copies = [
        pltpu.make_async_copy(down_hbm, down, sems.at[CHUNKS]),
        pltpu.make_async_copy(basis_hbm, basis, sems.at[CHUNKS + 1]),
        pltpu.make_async_copy(near_hbm, near, sems.at[CHUNKS + 2]),
    ]
    for copy in arriving:
        copy.start()
    low8 = low_lanes(8)
    low16, high16 = half_masks(16)

    def unpack(o, _):
        for s in range(SLOTS):
            at = pl.multiple_of((o * SLOTS + s) * 8, 8)
            values[pl.ds(at, 8), :] = got[o * TILES + s].astype(f32)
        at = pl.multiple_of(o * SLOTS, 8)
        target[pl.ds(at, 8), :] = got[o * TILES + SLOTS + 1].astype(f32)
        return 0

    for c in range(CHUNKS):
        arriving[c].wait()
        if c == 0:
            for copy in copies:
                copy.start()
        lax.fori_loop(c * span, (c + 1) * span, unpack, 0, unroll=8)
    landing = jnp.concatenate(
        [target[128 * i : 128 * i + 128, :].T for i in range(SLOTS)], axis=1
    ).astype(bf16)
    for u in range(0, 8, 2):
        chosen = jnp.concatenate(
            [values[pl.ds(u + k, PEERS * SLOTS, stride=8), :] for k in range(2)], axis=1
        ).astype(bf16)
        found = mm(landing, chosen)
        far[128 * u : 128 * u + 128, :] = found[:, :128]
        far[128 * u + 128 : 128 * u + 256, :] = found[:, 128:]

    def doubled(tile):
        turned = swap(tile)
        return jnp.concatenate(
            [jnp.where(low8, tile, turned), jnp.where(low8, turned, tile)], axis=0
        )

    me = lax.axis_index("leaf").astype(jnp.int32)
    total = jnp.zeros((2 * NV, HALF), f32)
    for level in range(LEVELS):
        parts = []
        for x in range(2**level, 2 ** (level + 1)):
            tile = got[lax.bitwise_xor(me, x) * TILES + SLOTS].astype(f32)
            if len(parts) < 4:
                parts.append(tile)
            else:
                parts[x % 4] = parts[x % 4] + tile
        tile = parts[0]
        for part in parts[1:]:
            tile = tile + part
        high, rest = split(doubled(tile))
        total = total + mmt(jnp.concatenate([high, rest * low16], axis=0), top_ref[level])
    root = total[:NV] + total[NV:]
    high, rest = split(jnp.concatenate([root, root], axis=1))
    root = jnp.concatenate([high * low16, high * high16, rest * low16, rest * high16], axis=0)

    for copy in copies:
        copy.wait()
    zero = jnp.zeros((2 * NV, 128), bf16)
    for c in range(8):
        found = mmt(root, down[512 * c : 512 * c + 512, :])
        for half in range(2):
            block = found[16 * half : 16 * half + 16] + found[32 + 16 * half : 48 + 16 * half]
            pieces = []
            for k in range(4):
                leaf = 64 * half + 8 * c + 2 * k
                f0 = far[pl.ds(leaf, 8, stride=128), :]
                f1 = far[pl.ds(leaf + 1, 8, stride=128), :]
                gathered = jnp.concatenate(
                    [jnp.where(low8, f0, swap(f1)), jnp.where(low8, swap(f0), f1)], axis=0
                )
                hat = (block[:, 128 * k : 128 * k + 128] + gathered).astype(bf16)
                pieces.append(jnp.concatenate([hat * low16, hat * high16], axis=0))
            for k in range(0, 4, 2):
                leaf = 64 * half + 8 * c + 2 * k
                stacked = jnp.concatenate(
                    [
                        jnp.concatenate([pieces[k], zero], axis=1),
                        jnp.concatenate([zero, pieces[k + 1]], axis=1),
                    ],
                    axis=0,
                )
                weight = jnp.concatenate(
                    [
                        basis[32 * leaf : 32 * leaf + 64, :],
                        basis[32 * leaf + 64 : 32 * leaf + 128, :],
                    ],
                    axis=1,
                )
                part = mmt(stacked, weight)
                for m in range(2):
                    at = 64 * leaf + 128 * m
                    out_ref[:, at : at + 128] = (
                        jnp.concatenate(
                            [part[32 * m : 32 * m + 16], part[32 * m + 16 : 32 * m + 32]], axis=1
                        )
                        + near[:, at : at + 128]
                    )
    edge = jnp.zeros((NV, HALF), f32)
    out_ref[:, :128] += jnp.concatenate([mmt(before_ref[...], ends_ref[:, :HALF]), edge], axis=1)
    out_ref[:, 8064:] += jnp.concatenate(
        [edge, mmt(following_ref[...], ends_ref[:, HALF:])], axis=1
    )


def vmem():
    return pl.BlockSpec(memory_space=pltpu.VMEM)


def hbm():
    return pl.BlockSpec(memory_space=pltpu.HBM)


def params(mib):
    return pltpu.CompilerParams(vmem_limit_bytes=mib * MIB)


def shape(dims, dtype):
    return jax.ShapeDtypeStruct(dims, dtype)


def run_up(src, own, dst, x_vecs, basis, edges, top_edges, pairs):
    return pl.pallas_call(
        up_kernel,
        name="up",
        out_shape=(shape((PEERS * TILES, 8, 128), bf16), shape((8, 128), f32)),
        in_specs=[vmem(), vmem(), vmem(), vmem(), hbm(), hbm(), hbm(), hbm()],
        out_specs=(vmem(), vmem()),
        scratch_shapes=[
            pltpu.SMEM((PAIR_ROWS,), jnp.int32),
            pltpu.SMEM((PAIR_ROWS // 128, 128), jnp.int32),
            pltpu.VMEM((LEAF_DEV, FLAT), bf16),
            pltpu.VMEM((EDGE_ROWS, FLAT), f32),
            pltpu.VMEM((PAIR_ROWS, FLAT), bf16),
            pltpu.VMEM((1024, 128), f32),
            pltpu.VMEM((1024, 128), f32),
            pltpu.VMEM((512, 128), f32),
            pltpu.VMEM((512, 128), f32),
            pltpu.VMEM((64 * (LEVELS - 1), 128), f32),
            pltpu.VMEM((64, NV, 128), f32),
            pltpu.VMEM((64, NV, 128), f32),
            pltpu.VMEM((128, 64, 128), bf16),
            pltpu.VMEM((128, 64, 128), bf16),
            pltpu.VMEM((LEAF_DEV, NV, 128), bf16),
            pltpu.VMEM((PAIR_ROWS // 128, 128), jnp.int32),
            pltpu.SemaphoreType.DMA((9,)),
        ],
        compiler_params=params(60),
        cost_estimate=pl.CostEstimate(
            flops=10**9, bytes_accessed=12 * 10**6, transcendentals=0
        ),
    )(x_vecs, top_edges, own, dst, src, basis, edges, pairs)


def run_mid(after, xs, xe, near, basis, edges, top, couple):
    return pl.pallas_call(
        mid_kernel,
        name="mid",
        out_shape=(
            shape((NV, LEAF_DEV * LEAF), f32),
            shape((LEAF_DEV * RANK // 2, 128), bf16),
            shape((LEAF_DEV * LEAF // 2, 128), bf16),
            shape((LEVELS, RANK, 128), bf16),
            shape((LEAF, 128), bf16),
        ),
        in_specs=[vmem(), vmem(), vmem(), hbm(), hbm(), hbm(), vmem(), vmem()],
        out_specs=(vmem(), vmem(), vmem(), vmem(), vmem()),
        scratch_shapes=[
            pltpu.VMEM((LEAF_DEV, 3 * FLAT), bf16),
            pltpu.VMEM((LEAF_DEV, FLAT), bf16),
            pltpu.VMEM((EDGE_ROWS, FLAT), f32),
            pltpu.VMEM((1024, 128), f32),
            pltpu.VMEM((1024, 128), f32),
            pltpu.VMEM((64, 64, 128), f32),
            pltpu.VMEM((64, 64, 128), f32),
            pltpu.VMEM((128, 64, 128), bf16),
            pltpu.VMEM((128, 64, 128), bf16),
            pltpu.SemaphoreType.DMA((3,)),
        ],
        compiler_params=params(62),
        cost_estimate=pl.CostEstimate(
            flops=10**9, bytes_accessed=14 * 10**6, transcendentals=0
        ),
    )(after, xs, xe, near, basis, edges, top, couple)


def run_down(got, near, down, basis, top, ends, before, following):
    return pl.pallas_call(
        down_kernel,
        name="down",
        out_shape=shape((NV, LEAF_DEV * LEAF), f32),
        in_specs=[hbm(), hbm(), hbm(), hbm(), vmem(), vmem(), vmem(), vmem()],
        out_specs=vmem(),
        scratch_shapes=[
            pltpu.VMEM((PEERS * TILES, 8, 128), bf16),
            pltpu.VMEM((NV, LEAF_DEV * LEAF), f32),
            pltpu.VMEM((LEAF_DEV * RANK // 2, 128), bf16),
            pltpu.VMEM((LEAF_DEV * LEAF // 2, 128), bf16),
            pltpu.VMEM((PEERS * SLOTS * 8, 128), f32),
            pltpu.VMEM((PEERS * SLOTS, 128), f32),
            pltpu.VMEM((8 * LEAF_DEV, 128), f32),
            pltpu.SemaphoreType.DMA((CHUNKS + 3,)),
        ],
        compiler_params=params(59),
        cost_estimate=pl.CostEstimate(
            flops=10**9, bytes_accessed=8 * 10**6, transcendentals=0
        ),
    )(got, near, down, basis, top, ends, before, following)


def shards(
    x_vecs,
    leaf_basis,
    near_blocks,
    local_edges,
    top_edges,
    top_couple,
    couple_blocks,
    couple_src,
    couple_owner,
    couple_dst,
):
    top_flat = top_edges.reshape((LEVELS - 1) * 32, 128)
    outgoing, after = run_up(
        couple_src, couple_owner.reshape(PAIR_ROWS // 128, 128),
        couple_dst.reshape(PAIR_ROWS // 128, 128), x_vecs, leaf_basis, local_edges, top_flat,
        couple_blocks,
    )
    first, last, after = lax.optimization_barrier((x_vecs[:, :LEAF], x_vecs[:, -LEAF:], after))
    ahead = [(i, (i + 1) % PEERS) for i in range(PEERS)]
    back = [(target, source) for source, target in ahead]
    before = lax.ppermute(last, "leaf", ahead)
    following = lax.ppermute(first, "leaf", back)
    got = lax.all_to_all(
        outgoing.reshape(PEERS, TILES * 8, 128), "leaf", split_axis=0, concat_axis=0, tiled=True
    ).reshape(PEERS * TILES, 8, 128)
    fill = jnp.zeros((NV, LEAF), bf16)
    xs = jnp.concatenate([fill, x_vecs, fill], axis=1)
    xe = jnp.concatenate([x_vecs, fill, fill], axis=1)
    near, down, basis, tops, ends = run_mid(
        after, xs, xe, near_blocks, leaf_basis, local_edges, top_flat,
        top_couple.reshape(LEVELS * 32, 128),
    )
    return run_down(got, near, down, basis, tops, ends, before, following)


def solution(mesh):
    return jax.shard_map(
        shards,
        mesh=mesh,
        in_specs=(
            P(None, "leaf"),
            P("leaf", None),
            P("leaf", None),
            P("leaf", None),
            P("leaf", None, None),
            P("leaf", None, None),
            P("leaf", None),
            P("leaf"),
            P("leaf", None),
            P("leaf"),
        ),
        out_specs=P(None, "leaf"),
        check_vma=False,
    )
```
